512 devices in a mesh: tile: 32 (over y, x), tm: 16 (over z, core).
Axes of the slice: x: 4, y: 8, z: 8, core: 2. Of those that a mesh axis runs over, the one named last changes fastest.
Arguments:
- movie: bfloat16 [256, 256, 4096], P('tm', None, 'tile'), may hold values from -6 to 6
- omega: bfloat16 [2, 32, 32, 256], P(None, 'tile', None, 'tm'), may hold values from -0.375 to 0.375
- time_taps: bfloat16 [17], replicated, may hold values from 0.019897461 to 0.099609375
- space_taps: bfloat16 [17], replicated, may hold values from 0.099609375 to 0.29882812
Outputs:
- basis: float32 [32, 256, 4096], P(None, 'tm', 'tile')
- coefficients: float32 [2, 32, 32, 256], P(None, 'tile', None, 'tm')
The draws below stay inside these ranges and needn't reach their ends.
All inputs are finite; a program needn't handle non-finite values.
Results may differ from the reference program's by a relative error of at most 0.024.
Values may be sent and summed in bfloat16 or wider, within the bound.
A program may use at most 64 MiB of HBM per device.

```python
import math
import jax
import jax.numpy as jnp
from jax import lax

H = 128
W = 128
TY = 2
K = 32
RAD = 8
FR_DEV = 16
FRAMES = 256
ROWS = 256
X = 4096
N_TILE = 32
N_TM = 16


def level_of(key, dims, shards, smallest, high):
    level, own = 1.0, jax.random.fold_in(key, 6)
    for dim, blocks in shards:
        draws = jnp.exp(jax.random.uniform(jax.random.fold_in(own, dim), (blocks,), jnp.float32, smallest / len(shards), high / len(shards)))
        level = level * jnp.repeat(draws, dims[dim] // blocks).reshape([-1 if axis == dim else 1 for axis in range(len(dims))])
    return level


def scatter_about(rng, dims, deviation, reach, shards=(), kind=jnp.bfloat16):
    result = jax.random.normal(rng, dims, jnp.float32) * deviation
    if len(shards) > 0:
        result = level_of(rng, dims, shards, -0.22, 0.18) * result
    return jnp.clip(result, min=-reach, max=reach).astype(kind)


def setup_inputs(seed: int = 0) -> dict:
    seeds = jax.random.split(jax.random.key(seed), 5)
    return {
        "movie": scatter_about(seeds[0], (FRAMES, ROWS, X), 1.0, 6.0, ((0, 16), (2, 32))),
        "omega": scatter_about(seeds[1], (TY, N_TILE, K, FRAMES), FRAMES ** -0.5, 0.375, ((1, 32), (3, 16))),
        "time_taps": jnp.clip(jax.random.uniform(seeds[2], (2 * RAD + 1,), jnp.float32, 0.019897461, 0.099609375), 0.019897461, 0.099609375).astype(jnp.bfloat16),
        "space_taps": jnp.clip(jax.random.uniform(seeds[3], (2 * RAD + 1,), jnp.float32, 0.099609375, 0.29882812), 0.099609375, 0.29882812).astype(jnp.bfloat16),
    }


def smooth(field, tap_row, along):
    radius = (tap_row.shape[0] - 1) // 2
    extent = field.shape[along]
    widths = [(0, 0)] * field.ndim
    widths[along] = (radius, radius)
    padded = jnp.pad(field, widths)
    summed = jnp.zeros_like(field)
    for tap_index in range(tap_row.shape[0]):
        summed = summed + tap_row[tap_index] * lax.slice_in_dim(padded, tap_index, tap_index + extent, axis=along)
    return summed

def orthonormal(matrix):
    gram_block = jnp.dot(matrix, matrix.T, precision=lax.Precision.HIGHEST)
    factor_low = jnp.linalg.cholesky(gram_block)
    return jax.scipy.linalg.solve_triangular(factor_low, matrix, lower=True)

def block_sum(left_side, matrix):
    left_blocks = left_side.astype(jnp.float32).reshape(K, N_TM, FR_DEV)
    right_blocks = matrix.astype(jnp.float32).reshape(N_TM, FR_DEV, H * W)
    parts = jnp.einsum('kcf,cfp->ckp', left_blocks, right_blocks)
    return lax.optimization_barrier(jnp.sum(parts.astype(jnp.bfloat16).astype(jnp.float32), axis=0))

def one_tile(pair):
    omega_tile, matrix = pair
    sketch = block_sum(omega_tile, matrix)
    first = orthonormal(sketch).astype(jnp.bfloat16)
    loadings = jnp.dot(matrix.astype(jnp.float32), first.T.astype(jnp.float32), preferred_element_type=jnp.float32).astype(jnp.bfloat16)
    refined = block_sum(loadings.T, matrix)
    final = orthonormal(refined)
    coefficients = lax.dot_general(final.astype(jnp.bfloat16).astype(jnp.float32), matrix.astype(jnp.float32), (((1,), (1,)), ((), ())), preferred_element_type=jnp.float32)
    return ((final * math.sqrt(H * W)).reshape(K, H, W), coefficients)

def reference(movie, omega, time_taps, space_taps):
    time_row = time_taps.astype(jnp.float32)
    space_row = space_taps.astype(jnp.float32)

    def one_column(inputs):
        tile_index, omega_column = inputs
        start = (tile_index * W).astype(jnp.int32)
        centre = lax.dynamic_slice_in_dim(movie, start, W, 2)
        left_rim = lax.dynamic_slice_in_dim(movie, jnp.maximum(start - RAD, 0).astype(jnp.int32), RAD, 2)
        right_rim = lax.dynamic_slice_in_dim(movie, jnp.minimum(start + W, X - RAD).astype(jnp.int32), RAD, 2)
        left_rim = jnp.where(tile_index > 0, left_rim, jnp.zeros_like(left_rim))
        right_rim = jnp.where(tile_index < N_TILE - 1, right_rim, jnp.zeros_like(right_rim))
        extended = jnp.concatenate([left_rim, centre, right_rim], axis=2).astype(jnp.float32)
        temporal = (extended - smooth(extended, time_row, 0)).astype(jnp.bfloat16)
        temporal_f = temporal.astype(jnp.float32)
        smooth_x = jnp.zeros((FRAMES, ROWS, W), jnp.float32)
        for tap_index in range(2 * RAD + 1):
            smooth_x = smooth_x + space_row[tap_index] * temporal_f[:, :, tap_index:tap_index + W]
        smooth_x = smooth_x.astype(jnp.bfloat16).astype(jnp.float32)
        lowpass = smooth(smooth_x, space_row, 1)
        filtered = (temporal_f[:, :, RAD:RAD + W] - lowpass).astype(jnp.bfloat16)
        matrices = jnp.transpose(filtered.reshape(FRAMES, TY, H * W), (1, 0, 2))
        return lax.map(one_tile, (omega_column, matrices))
    bases, coefficients = lax.map(one_column, (jnp.arange(N_TILE, dtype=jnp.int32), jnp.transpose(omega, (1, 0, 2, 3))))
    basis = jnp.transpose(bases, (2, 1, 3, 0, 4)).reshape(K, ROWS, X)
    return (basis, jnp.transpose(coefficients, (1, 0, 2, 3)))
```

```python
import functools
import math

import jax
import jax.numpy as jnp
from jax import lax
from jax.experimental import pallas as pl
from jax.experimental.pallas import tpu as pltpu
from jax.sharding import PartitionSpec as P

MESH = pl.DeviceIdType.MESH
F32 = jnp.float32
BF16 = jnp.bfloat16
HIGHEST = lax.Precision.HIGHEST

N_TM = 16
HALF = 8
FR = 16
FRAMES = 256
ROWS = 256
SHARE = 16
W = 128
K = 32
RAD = 8
PIX = SHARE * W


def mm(a, b, **kw):
    return jnp.dot(a, b, preferred_element_type=F32, **kw)


def mm_nt(a, b, **kw):
    return lax.dot_general(a, b, (((1,), (1,)), ((), ())), preferred_element_type=F32, **kw)


def mm_tn(a, b, **kw):
    return lax.dot_general(a, b, (((0,), (0,)), ((), ())), preferred_element_type=F32, **kw)


def pieces(x, count):
    out = []
    for _ in range(count - 1):
        part = x.astype(BF16)
        out.append(part)
        x = x - part.astype(F32)
    out.append(x.astype(BF16))
    return out


def stacked(x, count, axis=0):
    return jnp.concatenate(pieces(x, count), axis=axis)


def fold(x, count):
    total = x[:K]
    for i in range(1, count):
        total = total + x[i * K : (i + 1) * K]
    return total


def fold_lanes(x, count):
    total = x[:, :K]
    for i in range(1, count):
        total = total + x[:, i * K : (i + 1) * K]
    return total


def iota(shape, dim):
    return lax.broadcasted_iota(jnp.int32, shape, dim)


def from_taps(taps, index):
    out = jnp.zeros(index.shape, F32)
    for k in range(2 * RAD + 1):
        out = jnp.where(index == k, taps[:, k : k + 1], out)
    return out


def gram(x3):
    return fold_lanes(fold(mm_nt(x3, x3), 3), 3)


def inverse_factor(g):
    lane = iota((K, 128), 1)
    row = iota((K, 128), 0)
    aug = jnp.concatenate([g, jnp.where(iota((K, K), 0) == iota((K, K), 1), 1.0, 0.0), jnp.zeros((K, 64), F32)], axis=1)
    pivots = jnp.zeros((K, 128), F32)
    for j in range(K):
        line = aug[j : j + 1, :]
        pivot = line[:, j : j + 1]
        column = jnp.where(row > j, aug[:, j : j + 1], 0.0)
        pivots = jnp.where(row == j, pivot, pivots)
        aug = aug - column * (line / pivot)
    return (aug * lax.rsqrt(pivots))[:, K : 2 * K]


def kernel(
    n_tile,
    movie_hbm, omega_ref, time_ref, space_ref,
    basis_ref, coef_ref,
    movie, far, packed, edge, turn, out_buf, seen, om_all,
    b_slots, g_slots, b_mine, g_mine, f_mine, f_slots, y_buf, r_buf,
    load_sem, halo_s, halo_r, s_s, s_r, om_s, om_r, b_s, b_r, g_s, g_r, f_s, f_r,
):
    tile = lax.axis_index("tile")
    me = lax.axis_index("tm")
    half = me // HALF
    place = me - half * HALF
    left = lax.rem(tile + n_tile - 1, n_tile)
    right = lax.rem(tile + 1, n_tile)

    load = pltpu.make_async_copy(movie_hbm, movie, load_sem)
    load.start()
    barrier = pltpu.get_barrier_semaphore()
    for k in (8, 7, 9, 6, 10, 5, 11, 4, 12, 3, 13, 2, 14, 1, 15):
        pl.semaphore_signal(barrier, inc=1, device_id=(tile, lax.rem(me + k, N_TM)), device_id_type=MESH)
    pl.semaphore_signal(barrier, inc=1, device_id=(left, me), device_id_type=MESH)
    pl.semaphore_signal(barrier, inc=1, device_id=(right, me), device_id_type=MESH)

    space = space_ref[...].astype(F32)
    load.wait()

    lane = iota((W, 256), 1)
    col = iota((W, 256), 0)
    base = jnp.where(lane < 128, jnp.where(col < RAD, col - lane, 1), jnp.where(col >= W - RAD, col + 8 - lane, 1))
    total = jnp.zeros((ROWS, 256), F32)
    for f in range(FR):
        pick = jnp.where(base == -8 * f, 1.0, 0.0).astype(BF16)
        total = total + mm(movie[f], pick)
    packed[0] = total[:, :128].astype(BF16)
    packed[1] = total[:, 128:].astype(BF16)

    pl.semaphore_wait(barrier, N_TM - 1 + 2)
    halo = []
    for side, target in ((0, left), (1, right)):
        copy = pltpu.make_async_remote_copy(
            src_ref=packed.at[side], dst_ref=edge.at[side], send_sem=halo_s.at[side], recv_sem=halo_r.at[side],
            device_id=(target, me), device_id_type=MESH,
        )
        copy.start()
        halo.append(copy)
    om_copies = []
    for k in range(1, N_TM):
        peer = lax.rem(me + k, N_TM)
        copy = pltpu.make_async_remote_copy(
            src_ref=omega_ref.at[peer // HALF], dst_ref=om_all.at[me],
            send_sem=om_s.at[peer], recv_sem=om_r.at[me], device_id=(tile, peer), device_id_type=MESH,
        )
        copy.start()
        om_copies.append((copy, peer))
    om_all[me] = omega_ref[half]

    down = from_taps(space, iota((ROWS, ROWS), 1) - iota((ROWS, ROWS), 0) + RAD).astype(BF16)
    across = from_taps(space, iota((W, W), 0) - iota((W, W), 1) + RAD).astype(BF16)
    for f in range(FR):
        mid = mm(down, movie[f]).astype(BF16)
        far[:, f * W : (f + 1) * W] = movie[f].astype(F32) - mm(mid, across)

    n_id = iota((256, W), 0)
    c_id = iota((256, W), 1)
    j_id = lax.rem(n_id, RAD)
    spread = from_taps(space, jnp.where(n_id < 128, 136, 0) + j_id - c_id)
    owner = lax.rem(n_id, 128) // RAD

    for side in range(2):
        halo[side].wait_recv()
    rim_right = jnp.where(tile < n_tile - 1, edge[0].astype(F32), 0.0).astype(BF16)
    rim_left = jnp.where(tile > 0, edge[1].astype(F32), 0.0).astype(BF16)
    rim = mm(down, jnp.concatenate([rim_right, rim_left], axis=1)).astype(BF16)
    for f in range(FR):
        w_f = jnp.where(owner == f, spread, 0.0).astype(BF16)
        far[:, f * W : (f + 1) * W] = far[:, f * W : (f + 1) * W] - mm(rim, w_f)

    s_copies = []
    for k in (8, 7, 9, 6, 10, 5, 11, 4, 12, 3, 13, 2, 14, 1, 15, 0):
        peer = lax.rem(me + k, N_TM)
        slot = k % 2
        block = far[pl.ds(pl.multiple_of(peer * SHARE, SHARE), SHARE), :]
        for f in range(FR):
            turn[slot, pl.ds(f, SHARE, stride=FR), :] = block[:, f * W : (f + 1) * W]
        frames = turn[slot].reshape(SHARE, FR, W).astype(BF16)
        window = pl.ds(pl.multiple_of(me * FR, FR), FR)
        if k == 0:
            seen[:, window, :] = frames
        else:
            out_buf[k] = frames
            copy = pltpu.make_async_remote_copy(
                src_ref=out_buf.at[k], dst_ref=seen.at[:, window, :],
                send_sem=s_s.at[peer], recv_sem=s_r.at[me], device_id=(tile, peer), device_id_type=MESH,
            )
            copy.start()
            s_copies.append((copy, peer))

    time = time_ref[...].astype(F32)
    low = from_taps(time, iota((FRAMES, FRAMES), 1) - iota((FRAMES, FRAMES), 0) + RAD).astype(BF16)
    for k in range(1, N_TM):
        source = lax.rem(me + k, N_TM)
        pltpu.make_async_remote_copy(
            src_ref=omega_ref.at[0], dst_ref=om_all.at[source], send_sem=om_s.at[source], recv_sem=om_r.at[source],
            device_id=(tile, source), device_id_type=MESH,
        ).wait_recv()
    om = om_all[...].reshape(FRAMES, K)
    probe = om.astype(F32).T - mm_tn(om, low)
    probe2 = stacked(probe, 2)

    for k in range(1, N_TM):
        source = lax.rem(me + k, N_TM)
        pltpu.make_async_remote_copy(
            src_ref=out_buf.at[k], dst_ref=seen.at[:, pl.ds(pl.multiple_of(source * FR, FR), FR), :],
            send_sem=s_s.at[source], recv_sem=s_r.at[source], device_id=(tile, source), device_id_type=MESH,
        ).wait_recv()

    def pair(i):
        return jnp.concatenate([seen[2 * i], seen[2 * i + 1]], axis=1)

    back = jnp.zeros((3 * K, FRAMES), F32)
    for i in range(SHARE // 2):
        block = pair(i)
        y3 = stacked(fold(mm(probe2, block), 2), 3)
        y_buf[:, i * 256 : (i + 1) * 256] = y3
        back = back + mm_nt(y3, block)
    y_gram = gram(y_buf[...])
    b_mine[...] = fold(back, 3).astype(BF16)
    for i in range(4):
        g_mine[:, i * K : (i + 1) * K] = y_gram[8 * i : 8 * i + 8, :]
    b_slots[place] = b_mine[...]
    g_slots[place] = g_mine[...]
    x_copies = []
    for k in (4, 3, 5, 2, 6, 1, 7):
        other = lax.rem(place + k, HALF)
        peer = half * HALF + other
        for src, dst, ss, rs in ((b_mine, b_slots, b_s, b_r), (g_mine, g_slots, g_s, g_r)):
            copy = pltpu.make_async_remote_copy(
                src_ref=src, dst_ref=dst.at[place], send_sem=ss.at[other], recv_sem=rs.at[place],
                device_id=(tile, peer), device_id_type=MESH,
            )
            copy.start()
            x_copies.append((copy, src, dst, ss, rs, other, peer))
    for copy, src, dst, ss, rs, other, peer in x_copies:
        pltpu.make_async_remote_copy(
            src_ref=src, dst_ref=dst.at[other], send_sem=ss.at[other], recv_sem=rs.at[other],
            device_id=(tile, peer), device_id_type=MESH,
        ).wait_recv()
    g_sum = g_slots[0]
    b_sum = b_slots[0].astype(F32)
    for i in range(1, HALF):
        g_sum = g_sum + g_slots[i]
        b_sum = b_sum + b_slots[i].astype(F32)
    first = inverse_factor(jnp.concatenate([g_sum[:, i * K : (i + 1) * K] for i in range(4)], axis=0))

    back = b_sum - fold(mm_nt(stacked(b_sum, 3), low), 3)
    loads = mm(first, back, precision=HIGHEST).astype(BF16)
    probe2 = stacked(loads.astype(F32) - mm(loads, low), 2)
    down_p = jnp.zeros((FRAMES, 2 * K), F32)
    for i in range(SHARE // 2):
        block = pair(i)
        r = fold(mm(probe2, block), 2)
        r_buf[:, i * 256 : (i + 1) * 256] = r
        r3 = stacked(r, 3)
        y_buf[:, i * 256 : (i + 1) * 256] = r3
        down_p = down_p + mm_nt(block, r3[: 2 * K])
    r_gram = gram(y_buf[...])
    moved = fold_lanes(down_p, 2)
    moved = moved - fold_lanes(mm(low, stacked(moved, 2, axis=1)), 2)
    f_mine[:, :, 0:K] = moved.reshape(N_TM, FR, K)
    f_mine[:, :, K : 2 * K] = jnp.broadcast_to(r_gram[:FR][None], (N_TM, FR, K))
    f_mine[:, :, 2 * K : 3 * K] = jnp.broadcast_to(r_gram[FR:][None], (N_TM, FR, K))
    f_mine[:, :, 3 * K :] = jnp.zeros((N_TM, FR, K), F32)
    f_slots[me] = f_mine[me]
    for k in (8, 7, 9, 6, 10, 5, 11, 4, 12, 3, 13, 2, 14, 1, 15):
        peer = lax.rem(me + k, N_TM)
        pltpu.make_async_remote_copy(
            src_ref=f_mine.at[peer], dst_ref=f_slots.at[me], send_sem=f_s.at[peer], recv_sem=f_r.at[me],
            device_id=(tile, peer), device_id_type=MESH,
        ).start()
    for k in range(1, N_TM):
        source = lax.rem(me + k, N_TM)
        pltpu.make_async_remote_copy(
            src_ref=f_mine.at[source], dst_ref=f_slots.at[source], send_sem=f_s.at[source], recv_sem=f_r.at[source],
            device_id=(tile, source), device_id_type=MESH,
        ).wait()
    factors = []
    for s in range(2):
        total = f_slots[s * HALF]
        for i in range(1, HALF):
            total = total + f_slots[s * HALF + i]
        inverse = inverse_factor(jnp.concatenate([total[:, K : 2 * K], total[:, 2 * K : 3 * K]], axis=0))
        factors.append(inverse)
        coef_ref[s] = mm_nt(total[:, :K], inverse, precision=HIGHEST)
    final = jnp.where(half == 0, factors[0], factors[1]) * math.sqrt(ROWS // 2 * W)
    for i in range(SHARE // 2):
        two = mm(final, r_buf[:, i * 256 : (i + 1) * 256], precision=HIGHEST)
        for j in range(2):
            basis_ref[pl.ds(2 * i + j, K, stride=SHARE), :] = two[:, j * W : (j + 1) * W]

    for copy in halo:
        copy.wait_send()
    for copy, _ in om_copies:
        copy.wait_send()
    for copy, _ in s_copies:
        copy.wait_send()
    for entry in x_copies:
        entry[0].wait_send()


def solution(mesh):
    n_tile = mesh.shape["tile"]

    def local(movie, omega, time_taps, space_taps):
        dma = pltpu.SemaphoreType.DMA
        vmem = pl.BlockSpec(memory_space=pltpu.VMEM)
        basis, coef = pl.pallas_call(
            functools.partial(kernel, n_tile),
            out_shape=(
                jax.ShapeDtypeStruct((K * SHARE, W), F32),
                jax.ShapeDtypeStruct((2, FR, K), F32),
            ),
            in_specs=[pl.BlockSpec(memory_space=pl.ANY), vmem, vmem, vmem],
            out_specs=(vmem, vmem),
            scratch_shapes=[
                pltpu.VMEM((FR, ROWS, W), BF16),
                pltpu.VMEM((ROWS, FR * W), F32),
                pltpu.VMEM((2, ROWS, W), BF16),
                pltpu.VMEM((2, ROWS, W), BF16),
                pltpu.VMEM((2, SHARE * FR, W), F32),
                pltpu.VMEM((N_TM, SHARE, FR, W), BF16),
                pltpu.VMEM((SHARE, FRAMES, W), BF16),
                pltpu.VMEM((N_TM, FR, K), BF16),
                pltpu.VMEM((HALF, K, FRAMES), BF16),
                pltpu.VMEM((HALF, 8, 128), F32),
                pltpu.VMEM((K, FRAMES), BF16),
                pltpu.VMEM((8, 128), F32),
                pltpu.VMEM((N_TM, FR, 128), F32),
                pltpu.VMEM((N_TM, FR, 128), F32),
                pltpu.VMEM((3 * K, PIX), BF16),
                pltpu.VMEM((K, PIX), F32),
                dma(()), dma((2,)), dma((2,)), dma((N_TM,)), dma((N_TM,)), dma((N_TM,)), dma((N_TM,)),
                dma((HALF,)), dma((HALF,)), dma((HALF,)), dma((HALF,)), dma((N_TM,)), dma((N_TM,)),
            ],
            compiler_params=pltpu.CompilerParams(collective_id=0, has_side_effects=True),
            name="low_rank",
        )(
            movie,
            jnp.transpose(omega[:, 0], (0, 2, 1)),
            time_taps.reshape(1, -1),
            space_taps.reshape(1, -1),
        )
        return basis.reshape(K, SHARE, W), jnp.transpose(coef, (0, 2, 1))[:, None]

    in_specs = (P("tm", None, "tile"), P(None, "tile", None, "tm"), P(), P())
    out_specs = (P(None, "tm", "tile"), P(None, "tile", None, "tm"))
    return jax.shard_map(local, mesh=mesh, in_specs=in_specs, out_specs=out_specs, check_vma=False)
```

```python
import functools
import math

import jax
import jax.numpy as jnp
from jax import lax
from jax.experimental import pallas as pl
from jax.experimental.pallas import tpu as pltpu
from jax.sharding import PartitionSpec as P

MESH = pl.DeviceIdType.MESH
F32 = jnp.float32
BF16 = jnp.bfloat16
HIGHEST = lax.Precision.HIGHEST

N_TM = 16
HALF = 8
FR = 16
FRAMES = 256
ROWS = 256
SHARE = 16
W = 128
K = 32
RAD = 8
PIX = SHARE * W


def mm(a, b, **kw):
    return jnp.dot(a, b, preferred_element_type=F32, **kw)


def mm_nt(a, b, **kw):
    return lax.dot_general(a, b, (((1,), (1,)), ((), ())), preferred_element_type=F32, **kw)


def mm_tn(a, b, **kw):
    return lax.dot_general(a, b, (((0,), (0,)), ((), ())), preferred_element_type=F32, **kw)


def pieces(x, count):
    out = []
    for _ in range(count - 1):
        part = x.astype(BF16)
        out.append(part)
        x = x - part.astype(F32)
    out.append(x.astype(BF16))
    return out


def stacked(x, count, axis=0):
    return jnp.concatenate(pieces(x, count), axis=axis)


def fold(x, count):
    total = x[:K]
    for i in range(1, count):
        total = total + x[i * K : (i + 1) * K]
    return total


def fold_lanes(x, count):
    total = x[:, :K]
    for i in range(1, count):
        total = total + x[:, i * K : (i + 1) * K]
    return total


def iota(shape, dim):
    return lax.broadcasted_iota(jnp.int32, shape, dim)


def from_taps(taps, index):
    out = jnp.zeros(index.shape, F32)
    for k in range(2 * RAD + 1):
        out = jnp.where(index == k, taps[:, k : k + 1], out)
    return out


def gram(x3):
    return fold_lanes(fold(mm_nt(x3, x3), 3), 3)


def inverse_factors(grams):
    row = iota((8, 128), 0)
    eye = jnp.where(iota((K, K), 0) == iota((K, K), 1), 1.0, 0.0)
    state = []
    for g in grams:
        aug = jnp.concatenate([g, eye, jnp.zeros((K, 64), F32)], axis=1)
        state.append(([aug[8 * i : 8 * i + 8] for i in range(4)], []))
    for b in range(4):
        spread = [
            [[jnp.broadcast_to(aug[i][:, 8 * b + t : 8 * b + t + 1], (8, 128)) for i in range(b, 4)] for t in range(8)]
            for aug, _ in state
        ]
        scale = [jnp.ones((8, 128), F32) for _ in state]
        for t in range(8):
            for n, (aug, _) in enumerate(state):
                cols = spread[n]
                pivot = cols[t][0][t : t + 1, :]
                inverse = 1.0 / pivot
                scale[n] = jnp.where(row == t, pivot, scale[n])
                line = aug[b][t : t + 1, :] * inverse
                heads = [cols[u][0][t : t + 1, :] * inverse for u in range(t + 1, 8)]
                for i in range(b, 4):
                    factor = cols[t][i - b]
                    if i == b:
                        factor = jnp.where(row > t, factor, 0.0)
                    aug[i] = aug[i] - factor * line
                    for u in range(t + 1, 8):
                        cols[u][i - b] = cols[u][i - b] - factor * heads[u - t - 1]
        for n, (aug, done) in enumerate(state):
            done.append(aug[b] * lax.rsqrt(scale[n]))
    return [jnp.concatenate(done, axis=0)[:, K : 2 * K] for _, done in state]


def toeplitz(taps, size, flip):
    lane, row = iota((8, size), 1), iota((8, size), 0)
    head = from_taps(taps, row + 2 * RAD - lane if flip else lane - row)
    rows = []
    for i in range(size // 8):
        block = head
        if i == 0:
            block = jnp.where(lane >= 8, head, 0.0)
        if i == size // 8 - 1:
            block = jnp.where(lane < 16, head, 0.0)
        shift = (8 * i - 8) % size
        rows.append(pltpu.roll(block, shift, 1) if shift else block)
    return jnp.concatenate(rows, axis=0).astype(BF16)


def zeros16(*shape):
    return jnp.zeros(shape, BF16)


def pack_gram(ref, g):
    for i in range(4):
        ref[:, i * K : (i + 1) * K] = g[8 * i : 8 * i + 8, :]


def unpack_gram(total):
    return jnp.concatenate([total[:, i * K : (i + 1) * K] for i in range(4)], axis=0)


def kernel(
    n_tile,
    movie_hbm, omega_hbm, time_hbm, space_hbm,
    basis_ref, coef_ref,
    movie, omega_ref, time_ref, space_ref, far, packed, edge, turn, out_buf, seen, om_all,
    b_slots, g_slots, b_mine, g_mine, h_mine, h_slots, d_mine, d_slots, y_buf, r_buf,
    load_sem, halo_s, halo_r, s_s, s_r, om_s, om_r, b_s, b_r, g_s, g_r, h_s, h_r, d_s, d_r,
):
    tile = lax.axis_index("tile")
    me = lax.axis_index("tm")
    half = me // HALF
    place = me - half * HALF
    left = lax.rem(tile + n_tile - 1, n_tile)
    right = lax.rem(tile + 1, n_tile)
    far_first = (8, 7, 9, 6, 10, 5, 11, 4, 12, 3, 13, 2, 14, 1, 15)

    loads = [
        pltpu.make_async_copy(src, dst, load_sem.at[i])
        for i, (src, dst) in enumerate(
            ((movie_hbm, movie), (space_hbm, space_ref), (time_hbm, time_ref), (omega_hbm, omega_ref))
        )
    ]
    for load in loads:
        load.start()
    barrier = pltpu.get_barrier_semaphore()
    for k in far_first:
        pl.semaphore_signal(barrier, inc=1, device_id=(tile, lax.rem(me + k, N_TM)), device_id_type=MESH)
    pl.semaphore_signal(barrier, inc=1, device_id=(left, me), device_id_type=MESH)
    pl.semaphore_signal(barrier, inc=1, device_id=(right, me), device_id_type=MESH)

    loads[1].wait()
    space = space_ref[...].astype(F32)
    down = toeplitz(space, ROWS, False)
    side = toeplitz(space, W, True)
    across = jnp.concatenate(
        [jnp.concatenate([side, zeros16(W, W)], axis=1), jnp.concatenate([zeros16(W, W), side], axis=1)], axis=0
    )
    lane8, row8 = iota((8, W), 1), iota((8, W), 0)
    none8 = jnp.zeros((8, W), F32)
    rims = []
    for offset in (136, 0):
        one = from_taps(space, offset + row8 - lane8)
        rims.append(
            jnp.concatenate(
                [jnp.concatenate([one, none8], axis=1), jnp.concatenate([none8, one], axis=1)], axis=0
            ).astype(BF16)
        )
    unit = jnp.where(lane8 == row8, 1.0, 0.0)
    picks = []
    for f in range(FR):
        moved = pltpu.roll(unit, 8 * f, 1) if f else unit
        top = jnp.concatenate([moved, none8], axis=0).astype(BF16)
        bottom = jnp.concatenate([none8, moved], axis=0).astype(BF16)
        picks.append(jnp.concatenate([top, zeros16(16, W)], axis=1))
        picks.append(zeros16(W - 32, 2 * W))
        picks.append(jnp.concatenate([zeros16(16, W), bottom], axis=1))
    loads[0].wait()

    def frames2(g):
        return jnp.concatenate([movie[2 * g], movie[2 * g + 1]], axis=1)

    total = mm(jnp.concatenate([movie[f] for f in range(FR)], axis=1), jnp.concatenate(picks, axis=0))
    packed[0] = total[:, :W].astype(BF16)
    packed[1] = total[:, W:].astype(BF16)

    pl.semaphore_wait(barrier, N_TM - 1 + 2)
    halo = []
    for i, target in ((0, left), (1, right)):
        copy = pltpu.make_async_remote_copy(
            src_ref=packed.at[i], dst_ref=edge.at[i], send_sem=halo_s.at[i], recv_sem=halo_r.at[i],
            device_id=(target, me), device_id_type=MESH,
        )
        copy.start()
        halo.append(copy)

    for g in range(FR // 2):
        two = frames2(g)
        mid = mm(down, two).astype(BF16)
        far[:, 2 * g * W : 2 * (g + 1) * W] = two.astype(F32) - mm(mid, across)

    loads[2].wait()
    loads[3].wait()
    om_copies = []
    for k in far_first:
        peer = lax.rem(me + k, N_TM)
        copy = pltpu.make_async_remote_copy(
            src_ref=omega_ref.at[peer // HALF], dst_ref=om_all.at[me],
            send_sem=om_s.at[peer], recv_sem=om_r.at[me], device_id=(tile, peer), device_id_type=MESH,
        )
        copy.start()
        om_copies.append((copy, peer))
    om_all[me] = omega_ref[half]

    for i in range(2):
        halo[i].wait_recv()
    rim_right = jnp.where(tile < n_tile - 1, edge[0].astype(F32), 0.0).astype(BF16)
    rim_left = jnp.where(tile > 0, edge[1].astype(F32), 0.0).astype(BF16)
    rim = mm(down, jnp.concatenate([rim_right, rim_left], axis=1)).astype(BF16)
    for g in range(FR // 2):
        rows = []
        for i in range(2):
            rows += [zeros16(16 * g, 2 * W)] if g else []
            rows += [rims[i]]
            rows += [zeros16(W - 16 * g - 16, 2 * W)] if g < FR // 2 - 1 else []
        window = slice(2 * g * W, 2 * (g + 1) * W)
        far[:, window] = far[:, window] - mm(rim, jnp.concatenate(rows, axis=0))

    s_copies = []
    for k in far_first + (0,):
        peer = lax.rem(me + k, N_TM)
        slot = k % 2
        block = far[pl.ds(pl.multiple_of(peer * SHARE, SHARE), SHARE), :]
        for f in range(FR):
            turn[slot, pl.ds(f, SHARE, stride=FR), :] = block[:, f * W : (f + 1) * W]
        frames = turn[slot].reshape(SHARE, FR, W).astype(BF16)
        window = pl.ds(pl.multiple_of(me * FR, FR), FR)
        if k == 0:
            seen[:, window, :] = frames
        else:
            out_buf[k] = frames
            copy = pltpu.make_async_remote_copy(
                src_ref=out_buf.at[k], dst_ref=seen.at[:, window, :],
                send_sem=s_s.at[peer], recv_sem=s_r.at[me], device_id=(tile, peer), device_id_type=MESH,
            )
            copy.start()
            s_copies.append((copy, peer))

    time = time_ref[...].astype(F32)
    low = toeplitz(time, FRAMES, False)
    for k in range(1, N_TM):
        source = lax.rem(me + k, N_TM)
        pltpu.make_async_remote_copy(
            src_ref=omega_ref.at[0], dst_ref=om_all.at[source], send_sem=om_s.at[source], recv_sem=om_r.at[source],
            device_id=(tile, source), device_id_type=MESH,
        ).wait_recv()
    om = om_all[...].reshape(FRAMES, K)
    probe = om.astype(F32).T - mm_tn(om, low)
    probe2 = stacked(probe, 2)

    for k in range(1, N_TM):
        source = lax.rem(me + k, N_TM)
        pltpu.make_async_remote_copy(
            src_ref=out_buf.at[k], dst_ref=seen.at[:, pl.ds(pl.multiple_of(source * FR, FR), FR), :],
            send_sem=s_s.at[source], recv_sem=s_r.at[source], device_id=(tile, source), device_id_type=MESH,
        ).wait_recv()

    def pair(i):
        return jnp.concatenate([seen[2 * i], seen[2 * i + 1]], axis=1)

    for i in range(SHARE // 2):
        y_buf[:, i * 256 : (i + 1) * 256] = stacked(fold(mm(probe2, pair(i)), 2), 3)
    pack_gram(g_mine, gram(y_buf[...]))
    x_copies = []

    def to_half(src, dst, ss, rs):
        dst[place] = src[...]
        for k in (4, 3, 5, 2, 6, 1, 7):
            other = lax.rem(place + k, HALF)
            copy = pltpu.make_async_remote_copy(
                src_ref=src, dst_ref=dst.at[place], send_sem=ss.at[other], recv_sem=rs.at[place],
                device_id=(tile, half * HALF + other), device_id_type=MESH,
            )
            copy.start()
            x_copies.append(copy)

    def from_half(src, dst, ss, rs):
        for k in range(1, HALF):
            other = lax.rem(place + k, HALF)
            pltpu.make_async_remote_copy(
                src_ref=src, dst_ref=dst.at[other], send_sem=ss.at[other], recv_sem=rs.at[other],
                device_id=(tile, half * HALF + other), device_id_type=MESH,
            ).wait_recv()

    to_half(g_mine, g_slots, g_s, g_r)
    back = jnp.zeros((3 * K, FRAMES), F32)
    for i in range(SHARE // 2):
        back = back + mm_nt(y_buf[:, i * 256 : (i + 1) * 256], pair(i))
    b_mine[...] = fold(back, 3).astype(BF16)
    to_half(b_mine, b_slots, b_s, b_r)
    from_half(g_mine, g_slots, g_s, g_r)
    g_sum = g_slots[0]
    for i in range(1, HALF):
        g_sum = g_sum + g_slots[i]
    first = inverse_factors([unpack_gram(g_sum)])[0]
    from_half(b_mine, b_slots, b_s, b_r)
    b_sum = b_slots[0].astype(F32)
    for i in range(1, HALF):
        b_sum = b_sum + b_slots[i].astype(F32)

    back = b_sum - fold(mm_nt(stacked(b_sum, 3), low), 3)
    loadings = mm(first, back, precision=HIGHEST).astype(BF16)
    probe2 = stacked(loadings.astype(F32) - mm(loadings, low), 2)
    for i in range(SHARE // 2):
        r = fold(mm(probe2, pair(i)), 2)
        r_buf[:, i * 256 : (i + 1) * 256] = r
        y_buf[:, i * 256 : (i + 1) * 256] = stacked(r, 3)
    pack_gram(h_mine, gram(y_buf[...]))

    def to_all(src, dst, ss, rs):
        for k in far_first:
            peer = lax.rem(me + k, N_TM)
            copy = pltpu.make_async_remote_copy(
                src_ref=src(peer), dst_ref=dst.at[me], send_sem=ss.at[peer], recv_sem=rs.at[me],
                device_id=(tile, peer), device_id_type=MESH,
            )
            copy.start()
            x_copies.append(copy)

    def from_all(src, dst, ss, rs):
        for k in range(1, N_TM):
            source = lax.rem(me + k, N_TM)
            pltpu.make_async_remote_copy(
                src_ref=src(source), dst_ref=dst.at[source], send_sem=ss.at[source], recv_sem=rs.at[source],
                device_id=(tile, source), device_id_type=MESH,
            ).wait_recv()

    to_all(lambda peer: h_mine, h_slots, h_s, h_r)
    h_slots[me] = h_mine[...]
    down_p = jnp.zeros((FRAMES, 2 * K), F32)
    for i in range(SHARE // 2):
        down_p = down_p + mm_nt(pair(i), y_buf[: 2 * K, i * 256 : (i + 1) * 256])
    moved = fold_lanes(down_p, 2)
    moved = moved - fold_lanes(mm(low, stacked(moved, 2, axis=1)), 2)
    d_mine[...] = moved.astype(BF16).reshape(N_TM, FR, K)
    to_all(lambda peer: d_mine.at[peer], d_slots, d_s, d_r)
    d_slots[me] = d_mine[me]
    from_all(lambda peer: h_mine, h_slots, h_s, h_r)
    grams = []
    for s in range(2):
        total = h_slots[s * HALF]
        for i in range(1, HALF):
            total = total + h_slots[s * HALF + i]
        grams.append(unpack_gram(total))
    factors = inverse_factors(grams)
    final = jnp.where(half == 0, factors[0], factors[1])
    for i in range(SHARE // 2):
        two = mm(final, r_buf[:, i * 256 : (i + 1) * 256], precision=HIGHEST)
        for j in range(2):
            basis_ref[pl.ds(2 * i + j, K, stride=SHARE), :] = two[:, j * W : (j + 1) * W]
    from_all(lambda peer: d_mine.at[peer], d_slots, d_s, d_r)
    scale = 1.0 / math.sqrt(ROWS // 2 * W)
    for s in range(2):
        total = d_slots[s * HALF].astype(F32)
        for i in range(1, HALF):
            total = total + d_slots[s * HALF + i].astype(F32)
        coef_ref[s] = mm_nt(total, factors[s], precision=HIGHEST) * scale

    for copy in halo:
        copy.wait_send()
    for copy, _ in om_copies:
        copy.wait_send()
    for copy, _ in s_copies:
        copy.wait_send()
    for copy in x_copies:
        copy.wait_send()


def solution(mesh):
    n_tile = mesh.shape["tile"]

    def local(movie, omega, time_taps, space_taps):
        dma = pltpu.SemaphoreType.DMA
        vmem = pl.BlockSpec(memory_space=pltpu.VMEM)
        basis, coef = pl.pallas_call(
            functools.partial(kernel, n_tile),
            out_shape=(
                jax.ShapeDtypeStruct((K * SHARE, W), F32),
                jax.ShapeDtypeStruct((2, FR, K), F32),
            ),
            in_specs=[pl.BlockSpec(memory_space=pl.ANY)] * 4,
            out_specs=(vmem, vmem),
            scratch_shapes=[
                pltpu.VMEM((FR, ROWS, W), BF16),
                pltpu.VMEM((2, FR, K), BF16),
                pltpu.VMEM((1, 2 * RAD + 1), BF16),
                pltpu.VMEM((1, 2 * RAD + 1), BF16),
                pltpu.VMEM((ROWS, FR * W), F32),
                pltpu.VMEM((2, ROWS, W), BF16),
                pltpu.VMEM((2, ROWS, W), BF16),
                pltpu.VMEM((2, SHARE * FR, W), F32),
                pltpu.VMEM((N_TM, SHARE, FR, W), BF16),
                pltpu.VMEM((SHARE, FRAMES, W), BF16),
                pltpu.VMEM((N_TM, FR, K), BF16),
                pltpu.VMEM((HALF, K, FRAMES), BF16),
                pltpu.VMEM((HALF, 8, 128), F32),
                pltpu.VMEM((K, FRAMES), BF16),
                pltpu.VMEM((8, 128), F32),
                pltpu.VMEM((8, 128), F32),
                pltpu.VMEM((N_TM, 8, 128), F32),
                pltpu.VMEM((N_TM, FR, K), BF16),
                pltpu.VMEM((N_TM, FR, K), BF16),
                pltpu.VMEM((3 * K, PIX), BF16),
                pltpu.VMEM((K, PIX), F32),
                dma((4,)), dma((2,)), dma((2,)), dma((N_TM,)), dma((N_TM,)), dma((N_TM,)), dma((N_TM,)),
                dma((HALF,)), dma((HALF,)), dma((HALF,)), dma((HALF,)),
                dma((N_TM,)), dma((N_TM,)), dma((N_TM,)), dma((N_TM,)),
            ],
            compiler_params=pltpu.CompilerParams(collective_id=0, has_side_effects=True),
            name="low_rank",
        )(
            movie,
            jnp.transpose(omega[:, 0], (0, 2, 1)),
            time_taps.reshape(1, -1),
            space_taps.reshape(1, -1),
        )
        scale = math.sqrt(ROWS // 2 * W)
        return basis.reshape(K, SHARE, W) * scale, jnp.transpose(coef * scale, (0, 2, 1))[:, None]

    in_specs = (P("tm", None, "tile"), P(None, "tile", None, "tm"), P(), P())
    out_specs = (P(None, "tm", "tile"), P(None, "tile", None, "tm"))
    return jax.shard_map(local, mesh=mesh, in_specs=in_specs, out_specs=out_specs, check_vma=False)
```

```python
import functools
import math

import jax
import jax.numpy as jnp
from jax import lax
from jax.experimental import pallas as pl
from jax.experimental.pallas import tpu as pltpu
from jax.sharding import PartitionSpec as P

MESH = pl.DeviceIdType.MESH
F32 = jnp.float32
BF16 = jnp.bfloat16
HIGHEST = lax.Precision.HIGHEST

N_TM = 16
HALF = 8
FR = 16
FRAMES = 256
ROWS = 256
SHARE = 16
W = 128
K = 32
RAD = 8
PIX = SHARE * W
EARLY = (8, 7)


def mm(a, b, **kw):
    return jnp.dot(a, b, preferred_element_type=F32, **kw)


def mm_nt(a, b, **kw):
    return lax.dot_general(a, b, (((1,), (1,)), ((), ())), preferred_element_type=F32, **kw)


def mm_tn(a, b, **kw):
    return lax.dot_general(a, b, (((0,), (0,)), ((), ())), preferred_element_type=F32, **kw)


def pieces(x, count):
    out = []
    for _ in range(count - 1):
        part = x.astype(BF16)
        out.append(part)
        x = x - part.astype(F32)
    out.append(x.astype(BF16))
    return out


def stacked(x, count, axis=0):
    return jnp.concatenate(pieces(x, count), axis=axis)


def fold(x, count):
    total = x[:K]
    for i in range(1, count):
        total = total + x[i * K : (i + 1) * K]
    return total


def fold_lanes(x, count):
    total = x[:, :K]
    for i in range(1, count):
        total = total + x[:, i * K : (i + 1) * K]
    return total


def iota(shape, dim):
    return lax.broadcasted_iota(jnp.int32, shape, dim)


def from_taps(taps, index):
    out = jnp.zeros(index.shape, F32)
    for k in range(2 * RAD + 1):
        out = jnp.where(index == k, taps[:, k : k + 1], out)
    return out


def gram(x3):
    return fold_lanes(fold(mm_nt(x3, x3), 3), 3)


def inverse_factors(grams):
    row = iota((8, 128), 0)
    eye = jnp.where(iota((K, K), 0) == iota((K, K), 1), 1.0, 0.0)
    state = []
    for g in grams:
        aug = jnp.concatenate([g, eye, jnp.zeros((K, 64), F32)], axis=1)
        state.append(([aug[8 * i : 8 * i + 8] for i in range(4)], []))
    for b in range(4):
        spread = [
            [[jnp.broadcast_to(aug[i][:, 8 * b + t : 8 * b + t + 1], (8, 128)) for i in range(b, 4)] for t in range(8)]
            for aug, _ in state
        ]
        scale = [jnp.ones((8, 128), F32) for _ in state]
        for t in range(8):
            for n, (aug, _) in enumerate(state):
                cols = spread[n]
                pivot = cols[t][0][t : t + 1, :]
                inverse = 1.0 / pivot
                scale[n] = jnp.where(row == t, pivot, scale[n])
                line = aug[b][t : t + 1, :] * inverse
                heads = [cols[u][0][t : t + 1, :] * inverse for u in range(t + 1, 8)]
                for i in range(b, 4):
                    factor = cols[t][i - b]
                    if i == b:
                        factor = jnp.where(row > t, factor, 0.0)
                    aug[i] = aug[i] - factor * line
                    for u in range(t + 1, 8):
                        cols[u][i - b] = cols[u][i - b] - factor * heads[u - t - 1]
        for n, (aug, done) in enumerate(state):
            done.append(aug[b] * lax.rsqrt(scale[n]))
    return [jnp.concatenate(done, axis=0)[:, K : 2 * K] for _, done in state]


def toeplitz(taps, size, flip):
    lane, row = iota((8, size), 1), iota((8, size), 0)
    head = from_taps(taps, row + 2 * RAD - lane if flip else lane - row)
    rows = []
    for i in range(size // 8):
        block = head
        if i == 0:
            block = jnp.where(lane >= 8, head, 0.0)
        if i == size // 8 - 1:
            block = jnp.where(lane < 16, head, 0.0)
        shift = (8 * i - 8) % size
        rows.append(pltpu.roll(block, shift, 1) if shift else block)
    return jnp.concatenate(rows, axis=0).astype(BF16)


def zeros16(*shape):
    return jnp.zeros(shape, BF16)


def pack_gram(ref, g):
    for i in range(4):
        ref[:, i * K : (i + 1) * K] = g[8 * i : 8 * i + 8, :]


def unpack_gram(total):
    return jnp.concatenate([total[:, i * K : (i + 1) * K] for i in range(4)], axis=0)


def kernel(
    n_tile,
    movie_hbm, omega_hbm, time_hbm, space_hbm,
    basis_ref, coef_ref,
    movie, omega_ref, om_mine, fix, rim_buf, share, time_ref, space_ref, far, packed, edge, turn, out_buf, seen, om_all,
    b_slots, g_slots, b_mine, g_mine, h_mine, h_slots, d_mine, d_slots, y_buf, r_buf,
    load_sem, halo_s, halo_r, s_s, s_r, om_s, om_r, c_s, c_r, b_s, b_r, g_s, g_r, h_s, h_r, d_s, d_r,
):
    tile = lax.axis_index("tile")
    me = lax.axis_index("tm")
    half = me // HALF
    place = me - half * HALF
    left = lax.rem(tile + n_tile - 1, n_tile)
    right = lax.rem(tile + 1, n_tile)
    far_first = (8, 7, 9, 6, 10, 5, 11, 4, 12, 3, 13, 2, 14, 1, 15)

    loads = [
        pltpu.make_async_copy(src, dst, load_sem.at[i])
        for i, (src, dst) in enumerate(
            ((movie_hbm, movie), (space_hbm, space_ref), (time_hbm, time_ref), (omega_hbm, omega_ref))
        )
    ]
    for load in loads:
        load.start()
    barrier = pltpu.get_barrier_semaphore()
    for k in far_first:
        pl.semaphore_signal(barrier, inc=1, device_id=(tile, lax.rem(me + k, N_TM)), device_id_type=MESH)
    pl.semaphore_signal(barrier, inc=1, device_id=(left, me), device_id_type=MESH)
    pl.semaphore_signal(barrier, inc=1, device_id=(right, me), device_id_type=MESH)

    loads[1].wait()
    space = space_ref[...].astype(F32)
    down = toeplitz(space, ROWS, False)
    side = toeplitz(space, W, True)
    across = jnp.concatenate(
        [jnp.concatenate([side, zeros16(W, W)], axis=1), jnp.concatenate([zeros16(W, W), side], axis=1)], axis=0
    )
    lane8, row8 = iota((8, W), 1), iota((8, W), 0)
    none8 = jnp.zeros((8, W), F32)
    rims = []
    for offset in (136, 0):
        one = from_taps(space, offset + row8 - lane8)
        rims.append(
            jnp.concatenate(
                [jnp.concatenate([one, none8], axis=1), jnp.concatenate([none8, one], axis=1)], axis=0
            ).astype(BF16)
        )
    unit = jnp.where(lane8 == row8, 1.0, 0.0)
    picks = []
    for f in range(FR):
        moved = pltpu.roll(unit, 8 * f, 1) if f else unit
        top = jnp.concatenate([moved, none8], axis=0).astype(BF16)
        bottom = jnp.concatenate([none8, moved], axis=0).astype(BF16)
        picks.append(jnp.concatenate([top, zeros16(16, W)], axis=1))
        picks.append(zeros16(W - 32, 2 * W))
        picks.append(jnp.concatenate([zeros16(16, W), bottom], axis=1))
    loads[0].wait()

    def frames2(g):
        return jnp.concatenate([movie[2 * g], movie[2 * g + 1]], axis=1)

    total = mm(jnp.concatenate([movie[f] for f in range(FR)], axis=1), jnp.concatenate(picks, axis=0))
    packed[0] = total[:, :W].astype(BF16)
    packed[1] = total[:, W:].astype(BF16)

    for g in range(FR // 2):
        two = frames2(g)
        mid = mm(down, two).astype(BF16)
        far[:, 2 * g * W : 2 * (g + 1) * W] = two.astype(F32) - mm(mid, across)


    def rows_of(values, slot):
        for f in range(FR):
            turn[slot, pl.ds(f, SHARE, stride=FR), :] = values[:, f * W : (f + 1) * W]
        return turn[slot].reshape(SHARE, FR, W)

    def rows_at(peer):
        return pl.ds(pl.multiple_of(peer * SHARE, SHARE), SHARE)

    s_copies = []

    def block_copy(k):
        peer = lax.rem(me + k, N_TM)
        return pltpu.make_async_remote_copy(
            src_ref=out_buf.at[k], dst_ref=seen.at[:, rows_at(me), :],
            send_sem=s_s.at[peer], recv_sem=s_r.at[me], device_id=(tile, peer), device_id_type=MESH,
        )

    for i, k in enumerate(EARLY):
        out_buf[k] = rows_of(far[rows_at(lax.rem(me + k, N_TM)), :], i % 2).astype(BF16)
    loads[2].wait()
    loads[3].wait()
    for i in range(2):
        some = omega_ref[i].astype(F32)
        om_mine[i] = jnp.concatenate([some[4 * a : 4 * a + 4] for a in range(4)], axis=1).astype(BF16)

    pl.semaphore_wait(barrier, N_TM - 1 + 2)
    halo = []
    for i, target in ((0, left), (1, right)):
        copy = pltpu.make_async_remote_copy(
            src_ref=packed.at[i], dst_ref=edge.at[i], send_sem=halo_s.at[i], recv_sem=halo_r.at[i],
            device_id=(target, me), device_id_type=MESH,
        )
        copy.start()
        halo.append(copy)
    for k in EARLY:
        s_copies.append(block_copy(k))
        s_copies[-1].start()
    om_copies = []
    for k in far_first:
        peer = lax.rem(me + k, N_TM)
        copy = pltpu.make_async_remote_copy(
            src_ref=om_mine.at[peer // HALF], dst_ref=om_all.at[me],
            send_sem=om_s.at[peer], recv_sem=om_r.at[me], device_id=(tile, peer), device_id_type=MESH,
        )
        copy.start()
        om_copies.append(copy)
    om_all[me] = om_mine[half]

    for i in range(2):
        halo[i].wait_recv()
    rim_right = jnp.where(tile < n_tile - 1, edge[0].astype(F32), 0.0).astype(BF16)
    rim_left = jnp.where(tile > 0, edge[1].astype(F32), 0.0).astype(BF16)
    rim = mm(down, jnp.concatenate([rim_right, rim_left], axis=1)).astype(BF16)
    rim_buf[...] = rim
    c_copies = []
    for i, k in enumerate(EARLY):
        peer = lax.rem(me + k, N_TM)
        copy = pltpu.make_async_remote_copy(
            src_ref=rim_buf.at[rows_at(peer), :], dst_ref=fix.at[i],
            send_sem=c_s.at[i], recv_sem=c_r.at[i], device_id=(tile, peer), device_id_type=MESH,
        )
        copy.start()
        c_copies.append(copy)

    def rim_matrix(g):
        rows = []
        for i in range(2):
            rows += [zeros16(16 * g, 2 * W)] if g else []
            rows += [rims[i]]
            rows += [zeros16(W - 16 * g - 16, 2 * W)] if g < FR // 2 - 1 else []
        return jnp.concatenate(rows, axis=0)

    for g in range(FR // 2):
        window = slice(2 * g * W, 2 * (g + 1) * W)
        far[:, window] = far[:, window] - mm(rim, rim_matrix(g))

    for k in far_first + (0,):
        if k in EARLY:
            continue
        block = rows_of(far[rows_at(lax.rem(me + k, N_TM)), :], k % 2).astype(BF16)
        if k == 0:
            seen[:, rows_at(me), :] = block
        else:
            out_buf[k] = block
            s_copies.append(block_copy(k))
            s_copies[-1].start()

    time = time_ref[...].astype(F32)
    low = toeplitz(time, FRAMES, False)
    for k in range(1, N_TM):
        source = lax.rem(me + k, N_TM)
        pltpu.make_async_remote_copy(
            src_ref=om_mine.at[0], dst_ref=om_all.at[source], send_sem=om_s.at[source], recv_sem=om_r.at[source],
            device_id=(tile, source), device_id_type=MESH,
        ).wait_recv()
    om = om_all[...].astype(F32).reshape(4 * N_TM, 128)
    om = jnp.concatenate([om[:, a * K : (a + 1) * K] for a in range(4)], axis=0).astype(BF16)
    n_id = iota((FRAMES, FRAMES), 0)
    at = lax.rem(n_id, 64) // 4 * FR + n_id // 64 * 4 + lax.rem(n_id, 4)
    om = mm_tn(om, jnp.where(at == iota((FRAMES, FRAMES), 1), 1.0, 0.0).astype(BF16))
    probe = om - mm(om.astype(BF16), low)
    probe2 = stacked(probe, 2)

    def block_wait(k):
        source = lax.rem(me + N_TM - k, N_TM)
        pltpu.make_async_remote_copy(
            src_ref=out_buf.at[k], dst_ref=seen.at[:, rows_at(source), :],
            send_sem=s_s.at[source], recv_sem=s_r.at[source], device_id=(tile, source), device_id_type=MESH,
        ).wait_recv()

    for copy in c_copies:
        copy.wait_recv()
    rims_in = fix[...].reshape(len(EARLY) * SHARE, 2 * W)
    for g in range(FR // 2):
        share[:, 2 * g * W : 2 * (g + 1) * W] = mm(rims_in, rim_matrix(g))
    for i, k in enumerate(EARLY):
        block_wait(k)
        window = rows_at(lax.rem(me + N_TM - k, N_TM))
        moved = rows_of(share[i * SHARE : (i + 1) * SHARE, :], i % 2)
        seen[:, window, :] = (seen[:, window, :].astype(F32) - moved).astype(BF16)
    for k in far_first:
        if k not in EARLY:
            block_wait(k)

    def pair(i):
        return jnp.concatenate([seen[2 * i], seen[2 * i + 1]], axis=1)

    for i in range(SHARE // 2):
        y_buf[:, i * 256 : (i + 1) * 256] = stacked(fold(mm(probe2, pair(i)), 2), 3)
    pack_gram(g_mine, gram(y_buf[...]))
    x_copies = []

    def to_half(src, dst, ss, rs):
        dst[place] = src[...]
        for k in (4, 3, 5, 2, 6, 1, 7):
            other = lax.rem(place + k, HALF)
            copy = pltpu.make_async_remote_copy(
                src_ref=src, dst_ref=dst.at[place], send_sem=ss.at[other], recv_sem=rs.at[place],
                device_id=(tile, half * HALF + other), device_id_type=MESH,
            )
            copy.start()
            x_copies.append(copy)

    def from_half(src, dst, ss, rs):
        for k in range(1, HALF):
            other = lax.rem(place + k, HALF)
            pltpu.make_async_remote_copy(
                src_ref=src, dst_ref=dst.at[other], send_sem=ss.at[other], recv_sem=rs.at[other],
                device_id=(tile, half * HALF + other), device_id_type=MESH,
            ).wait_recv()

    to_half(g_mine, g_slots, g_s, g_r)
    back = jnp.zeros((3 * K, FRAMES), F32)
    for i in range(SHARE // 2):
        back = back + mm_nt(y_buf[:, i * 256 : (i + 1) * 256], pair(i))
    b_mine[...] = fold(back, 3).astype(BF16)
    to_half(b_mine, b_slots, b_s, b_r)
    from_half(g_mine, g_slots, g_s, g_r)
    g_sum = g_slots[0]
    for i in range(1, HALF):
        g_sum = g_sum + g_slots[i]
    first = inverse_factors([unpack_gram(g_sum)])[0]
    from_half(b_mine, b_slots, b_s, b_r)
    b_sum = b_slots[0].astype(F32)
    for i in range(1, HALF):
        b_sum = b_sum + b_slots[i].astype(F32)

    back = b_sum - fold(mm_nt(stacked(b_sum, 3), low), 3)
    loadings = mm(first, back, precision=HIGHEST).astype(BF16)
    probe2 = stacked(loadings.astype(F32) - mm(loadings, low), 2)
    for i in range(SHARE // 2):
        r = fold(mm(probe2, pair(i)), 2)
        r_buf[:, i * 256 : (i + 1) * 256] = r
        y_buf[:, i * 256 : (i + 1) * 256] = stacked(r, 3)
    pack_gram(h_mine, gram(y_buf[...]))

    def to_all(src, dst, ss, rs):
        for k in far_first:
            peer = lax.rem(me + k, N_TM)
            copy = pltpu.make_async_remote_copy(
                src_ref=src(peer), dst_ref=dst.at[me], send_sem=ss.at[peer], recv_sem=rs.at[me],
                device_id=(tile, peer), device_id_type=MESH,
            )
            copy.start()
            x_copies.append(copy)

    def from_all(src, dst, ss, rs):
        for k in range(1, N_TM):
            source = lax.rem(me + k, N_TM)
            pltpu.make_async_remote_copy(
                src_ref=src(source), dst_ref=dst.at[source], send_sem=ss.at[source], recv_sem=rs.at[source],
                device_id=(tile, source), device_id_type=MESH,
            ).wait_recv()

    to_all(lambda peer: h_mine, h_slots, h_s, h_r)
    h_slots[me] = h_mine[...]
    down_p = jnp.zeros((FRAMES, 2 * K), F32)
    for i in range(SHARE // 2):
        down_p = down_p + mm_nt(pair(i), y_buf[: 2 * K, i * 256 : (i + 1) * 256])
    moved = fold_lanes(down_p, 2)
    moved = moved - fold_lanes(mm(low, stacked(moved, 2, axis=1)), 2)
    d_mine[...] = moved.astype(BF16).reshape(N_TM, FR, K)
    to_all(lambda peer: d_mine.at[peer], d_slots, d_s, d_r)
    d_slots[me] = d_mine[me]
    from_all(lambda peer: h_mine, h_slots, h_s, h_r)
    grams = []
    for s in range(2):
        total = h_slots[s * HALF]
        for i in range(1, HALF):
            total = total + h_slots[s * HALF + i]
        grams.append(unpack_gram(total))
    factors = inverse_factors(grams)
    final = jnp.where(half == 0, factors[0], factors[1]) * math.sqrt(ROWS // 2 * W)
    for i in range(SHARE // 2):
        two = mm(final, r_buf[:, i * 256 : (i + 1) * 256], precision=HIGHEST)
        for j in range(2):
            basis_ref[pl.ds(2 * i + j, K, stride=SHARE), :] = two[:, j * W : (j + 1) * W]
    from_all(lambda peer: d_mine.at[peer], d_slots, d_s, d_r)
    for s in range(2):
        total = d_slots[s * HALF].astype(F32)
        for i in range(1, HALF):
            total = total + d_slots[s * HALF + i].astype(F32)
        coef_ref[s] = mm_nt(total, factors[s], precision=HIGHEST)

    for copy in halo:
        copy.wait_send()
    for copy in om_copies + s_copies + c_copies:
        copy.wait_send()
    for copy in x_copies:
        copy.wait_send()


def solution(mesh):
    n_tile = mesh.shape["tile"]

    def local(movie, omega, time_taps, space_taps):
        dma = pltpu.SemaphoreType.DMA
        vmem = pl.BlockSpec(memory_space=pltpu.VMEM)
        basis, coef = pl.pallas_call(
            functools.partial(kernel, n_tile),
            out_shape=(
                pltpu.VMEM((K * SHARE, W), F32),
                pltpu.VMEM((2, FR, K), F32),
            ),
            in_specs=[pl.BlockSpec(memory_space=pl.ANY)] * 4,
            out_specs=(vmem, vmem),
            scratch_shapes=[
                pltpu.VMEM((FR, ROWS, W), BF16),
                pltpu.VMEM((2, FR, K), BF16),
                pltpu.VMEM((2, 4, 4 * K), BF16),
                pltpu.VMEM((len(EARLY), SHARE, 2 * W), BF16),
                pltpu.VMEM((ROWS, 2 * W), BF16),
                pltpu.VMEM((len(EARLY) * SHARE, FR * W), F32),
                pltpu.VMEM((1, 2 * RAD + 1), BF16),
                pltpu.VMEM((1, 2 * RAD + 1), BF16),
                pltpu.VMEM((ROWS, FR * W), F32),
                pltpu.VMEM((2, ROWS, W), BF16),
                pltpu.VMEM((2, ROWS, W), BF16),
                pltpu.VMEM((2, SHARE * FR, W), F32),
                pltpu.VMEM((N_TM, SHARE, FR, W), BF16),
                pltpu.VMEM((SHARE, FRAMES, W), BF16),
                pltpu.VMEM((N_TM, 4, 4 * K), BF16),
                pltpu.VMEM((HALF, K, FRAMES), BF16),
                pltpu.VMEM((HALF, 8, 128), F32),
                pltpu.VMEM((K, FRAMES), BF16),
                pltpu.VMEM((8, 128), F32),
                pltpu.VMEM((8, 128), F32),
                pltpu.VMEM((N_TM, 8, 128), F32),
                pltpu.VMEM((N_TM, FR, K), BF16),
                pltpu.VMEM((N_TM, FR, K), BF16),
                pltpu.VMEM((3 * K, PIX), BF16),
                pltpu.VMEM((K, PIX), F32),
                dma((4,)), dma((2,)), dma((2,)), dma((N_TM,)), dma((N_TM,)), dma((N_TM,)), dma((N_TM,)),
                dma((len(EARLY),)), dma((len(EARLY),)),
                dma((HALF,)), dma((HALF,)), dma((HALF,)), dma((HALF,)),
                dma((N_TM,)), dma((N_TM,)), dma((N_TM,)), dma((N_TM,)),
            ],
            compiler_params=pltpu.CompilerParams(collective_id=0, has_side_effects=True),
            name="low_rank",
        )(
            movie,
            jnp.transpose(omega[:, 0], (0, 2, 1)),
            time_taps.reshape(1, -1),
            space_taps.reshape(1, -1),
        )
        return basis.reshape(K, SHARE, W), jnp.transpose(coef, (0, 2, 1))[:, None]

    in_specs = (P("tm", None, "tile"), P(None, "tile", None, "tm"), P(), P())
    out_specs = (P(None, "tm", "tile"), P(None, "tile", None, "tm"))
    return jax.shard_map(local, mesh=mesh, in_specs=in_specs, out_specs=out_specs, check_vma=False)
```

```python
import functools
import math

import jax
import jax.numpy as jnp
from jax import lax
from jax.experimental import pallas as pl
from jax.experimental.pallas import tpu as pltpu
from jax.sharding import PartitionSpec as P

MESH = pl.DeviceIdType.MESH
F32 = jnp.float32
BF16 = jnp.bfloat16
HIGHEST = lax.Precision.HIGHEST

N_TM = 16
HALF = 8
FR = 16
FRAMES = 256
ROWS = 256
SHARE = 16
W = 128
K = 32
RAD = 8
PIX = SHARE * W
EARLY = (8, 7)


def mm(a, b, **kw):
    return jnp.dot(a, b, preferred_element_type=F32, **kw)


def mm_nt(a, b, **kw):
    return lax.dot_general(a, b, (((1,), (1,)), ((), ())), preferred_element_type=F32, **kw)


def mm_tn(a, b, **kw):
    return lax.dot_general(a, b, (((0,), (0,)), ((), ())), preferred_element_type=F32, **kw)


def pieces(x, count):
    out = []
    for _ in range(count - 1):
        part = x.astype(BF16)
        out.append(part)
        x = x - part.astype(F32)
    out.append(x.astype(BF16))
    return out


def stacked(x, count, axis=0):
    return jnp.concatenate(pieces(x, count), axis=axis)


def fold(x, count):
    total = x[:K]
    for i in range(1, count):
        total = total + x[i * K : (i + 1) * K]
    return total


def fold_lanes(x, count):
    total = x[:, :K]
    for i in range(1, count):
        total = total + x[:, i * K : (i + 1) * K]
    return total


def iota(shape, dim):
    return lax.broadcasted_iota(jnp.int32, shape, dim)


def from_taps(taps, index):
    out = jnp.zeros(index.shape, F32)
    for k in range(2 * RAD + 1):
        out = jnp.where(index == k, taps[:, k : k + 1], out)
    return out


def gram(x2):
    return fold_lanes(fold(mm_nt(x2, x2), 2), 2)


def inverse_factors(grams):
    row = iota((8, 128), 0)
    eye = jnp.where(iota((K, K), 0) == iota((K, K), 1), 1.0, 0.0)
    state = []
    for g in grams:
        aug = jnp.concatenate([g, eye, jnp.zeros((K, 64), F32)], axis=1)
        state.append(([aug[8 * i : 8 * i + 8] for i in range(4)], []))
    for b in range(4):
        spread = [
            [[jnp.broadcast_to(aug[i][:, 8 * b + t : 8 * b + t + 1], (8, 128)) for i in range(b, 4)] for t in range(8)]
            for aug, _ in state
        ]
        scale = [jnp.ones((8, 128), F32) for _ in state]
        for t in range(8):
            for n, (aug, _) in enumerate(state):
                cols = spread[n]
                pivot = cols[t][0][t : t + 1, :]
                inverse = 1.0 / pivot
                scale[n] = jnp.where(row == t, pivot, scale[n])
                line = aug[b][t : t + 1, :] * inverse
                heads = [cols[u][0][t : t + 1, :] * inverse for u in range(t + 1, 8)]
                for i in range(b, 4):
                    factor = cols[t][i - b]
                    if i == b:
                        factor = jnp.where(row > t, factor, 0.0)
                    aug[i] = aug[i] - factor * line
                    for u in range(t + 1, 8):
                        cols[u][i - b] = cols[u][i - b] - factor * heads[u - t - 1]
        for n, (aug, done) in enumerate(state):
            done.append(aug[b] * lax.rsqrt(scale[n]))
    return [jnp.concatenate(done, axis=0)[:, K : 2 * K] for _, done in state]


def toeplitz(taps, size, flip):
    lane, row = iota((8, size), 1), iota((8, size), 0)
    head = from_taps(taps, row + 2 * RAD - lane if flip else lane - row)
    rows = []
    for i in range(size // 8):
        block = head
        if i == 0:
            block = jnp.where(lane >= 8, head, 0.0)
        if i == size // 8 - 1:
            block = jnp.where(lane < 16, head, 0.0)
        shift = (8 * i - 8) % size
        rows.append(pltpu.roll(block, shift, 1) if shift else block)
    return jnp.concatenate(rows, axis=0).astype(BF16)


def zeros16(*shape):
    return jnp.zeros(shape, BF16)


def pack_gram(ref, g):
    for i in range(4):
        ref[:, i * K : (i + 1) * K] = g[8 * i : 8 * i + 8, :]


def unpack_rows(total):
    return jnp.concatenate([total[:, i * K : (i + 1) * K] for i in range(4)], axis=0)


def unpack_gram(total):
    return jnp.concatenate([total[:, i * K : (i + 1) * K] for i in range(4)], axis=0)


def kernel(
    n_tile,
    movie_hbm, omega_hbm, time_hbm, space_hbm,
    basis_ref, coef_ref,
    movie, omega_ref, om_mine, fix, rim_buf, share, time_ref, space_ref, far, packed, edge, turn, out_buf, seen, om_all,
    b_slots, g_slots, b_mine, g_mine, orders, h_mine, h_slots, d_mine, d_slots, y_buf, r_buf,
    load_sem, halo_s, halo_r, s_s, s_r, om_s, om_r, c_s, c_r, b_s, b_r, g_s, g_r, h_s, h_r, d_s, d_r,
):
    tile = lax.axis_index("tile")
    me = lax.axis_index("tm")
    half = me // HALF
    place = me - half * HALF
    left = lax.rem(tile + n_tile - 1, n_tile)
    right = lax.rem(tile + 1, n_tile)
    far_first = (8, 7, 9, 6, 10, 5, 11, 4, 12, 3, 13, 2, 14, 1, 15)

    loads = [
        pltpu.make_async_copy(src, dst, load_sem.at[i])
        for i, (src, dst) in enumerate(
            ((movie_hbm, movie), (space_hbm, space_ref), (time_hbm, time_ref), (omega_hbm, omega_ref))
        )
    ]
    for load in loads:
        load.start()
    barrier = pltpu.get_barrier_semaphore()
    for k in far_first:
        pl.semaphore_signal(barrier, inc=1, device_id=(tile, lax.rem(me + k, N_TM)), device_id_type=MESH)
    pl.semaphore_signal(barrier, inc=1, device_id=(left, me), device_id_type=MESH)
    pl.semaphore_signal(barrier, inc=1, device_id=(right, me), device_id_type=MESH)

    loads[1].wait()
    space = space_ref[...].astype(F32)
    down = toeplitz(space, ROWS, False)
    side = toeplitz(space, W, True)
    across = jnp.concatenate(
        [jnp.concatenate([side, zeros16(W, W)], axis=1), jnp.concatenate([zeros16(W, W), side], axis=1)], axis=0
    )
    lane8, row8 = iota((8, W), 1), iota((8, W), 0)
    none8 = jnp.zeros((8, W), F32)
    rims = []
    for offset in (136, 0):
        one = from_taps(space, offset + row8 - lane8)
        rims.append(
            jnp.concatenate(
                [jnp.concatenate([one, none8], axis=1), jnp.concatenate([none8, one], axis=1)], axis=0
            ).astype(BF16)
        )
    unit = jnp.where(lane8 == row8, 1.0, 0.0)
    picks = []
    for f in range(FR):
        moved = pltpu.roll(unit, 8 * f, 1) if f else unit
        top = jnp.concatenate([moved, none8], axis=0).astype(BF16)
        bottom = jnp.concatenate([none8, moved], axis=0).astype(BF16)
        picks.append(jnp.concatenate([top, zeros16(16, W)], axis=1))
        picks.append(zeros16(W - 32, 2 * W))
        picks.append(jnp.concatenate([zeros16(16, W), bottom], axis=1))
    loads[0].wait()

    def frames2(g):
        return jnp.concatenate([movie[2 * g], movie[2 * g + 1]], axis=1)

    total = mm(jnp.concatenate([movie[f] for f in range(FR)], axis=1), jnp.concatenate(picks, axis=0))
    packed[0] = total[:, :W].astype(BF16)
    packed[1] = total[:, W:].astype(BF16)

    for g in range(FR // 2):
        two = frames2(g)
        mid = mm(down, two).astype(BF16)
        far[:, 2 * g * W : 2 * (g + 1) * W] = two.astype(F32) - mm(mid, across)


    def rows_of(values, slot):
        for f in range(FR):
            turn[slot, pl.ds(f, SHARE, stride=FR), :] = values[:, f * W : (f + 1) * W]
        return turn[slot].reshape(SHARE, FR, W)

    def rows_at(peer):
        return pl.ds(pl.multiple_of(peer * SHARE, SHARE), SHARE)

    s_copies = []

    def block_copy(k):
        peer = lax.rem(me + k, N_TM)
        return pltpu.make_async_remote_copy(
            src_ref=out_buf.at[k], dst_ref=seen.at[:, rows_at(me), :],
            send_sem=s_s.at[peer], recv_sem=s_r.at[me], device_id=(tile, peer), device_id_type=MESH,
        )

    for i, k in enumerate(EARLY):
        out_buf[k] = rows_of(far[rows_at(lax.rem(me + k, N_TM)), :], i % 2).astype(BF16)
    loads[2].wait()
    loads[3].wait()
    for i in range(2):
        some = omega_ref[i].astype(F32)
        om_mine[i] = jnp.concatenate([some[4 * a : 4 * a + 4] for a in range(4)], axis=1).astype(BF16)

    pl.semaphore_wait(barrier, N_TM - 1 + 2)
    halo = []
    for i, target in ((0, left), (1, right)):
        copy = pltpu.make_async_remote_copy(
            src_ref=packed.at[i], dst_ref=edge.at[i], send_sem=halo_s.at[i], recv_sem=halo_r.at[i],
            device_id=(target, me), device_id_type=MESH,
        )
        copy.start()
        halo.append(copy)
    for k in EARLY:
        s_copies.append(block_copy(k))
        s_copies[-1].start()
    om_copies = []
    for k in far_first:
        peer = lax.rem(me + k, N_TM)
        copy = pltpu.make_async_remote_copy(
            src_ref=om_mine.at[peer // HALF], dst_ref=om_all.at[me],
            send_sem=om_s.at[peer], recv_sem=om_r.at[me], device_id=(tile, peer), device_id_type=MESH,
        )
        copy.start()
        om_copies.append(copy)
    om_all[me] = om_mine[half]

    for i in range(2):
        halo[i].wait_recv()
    rim_right = jnp.where(tile < n_tile - 1, edge[0].astype(F32), 0.0).astype(BF16)
    rim_left = jnp.where(tile > 0, edge[1].astype(F32), 0.0).astype(BF16)
    rim = mm(down, jnp.concatenate([rim_right, rim_left], axis=1)).astype(BF16)
    rim_buf[...] = rim
    c_copies = []
    for i, k in enumerate(EARLY):
        peer = lax.rem(me + k, N_TM)
        copy = pltpu.make_async_remote_copy(
            src_ref=rim_buf.at[rows_at(peer), :], dst_ref=fix.at[i],
            send_sem=c_s.at[i], recv_sem=c_r.at[i], device_id=(tile, peer), device_id_type=MESH,
        )
        copy.start()
        c_copies.append(copy)

    def rim_matrix(g):
        rows = []
        for i in range(2):
            rows += [zeros16(16 * g, 2 * W)] if g else []
            rows += [rims[i]]
            rows += [zeros16(W - 16 * g - 16, 2 * W)] if g < FR // 2 - 1 else []
        return jnp.concatenate(rows, axis=0)

    for g in range(FR // 2):
        window = slice(2 * g * W, 2 * (g + 1) * W)
        far[:, window] = far[:, window] - mm(rim, rim_matrix(g))

    for k in far_first + (0,):
        if k in EARLY:
            continue
        block = rows_of(far[rows_at(lax.rem(me + k, N_TM)), :], k % 2).astype(BF16)
        if k == 0:
            seen[:, rows_at(me), :] = block
        else:
            out_buf[k] = block
            s_copies.append(block_copy(k))
            s_copies[-1].start()

    time = time_ref[...].astype(F32)
    low = toeplitz(time, FRAMES, False)
    for k in range(1, N_TM):
        source = lax.rem(me + k, N_TM)
        pltpu.make_async_remote_copy(
            src_ref=om_mine.at[0], dst_ref=om_all.at[source], send_sem=om_s.at[source], recv_sem=om_r.at[source],
            device_id=(tile, source), device_id_type=MESH,
        ).wait_recv()
    om = om_all[...].astype(F32).reshape(4 * N_TM, 128)
    om = jnp.concatenate([om[:, a * K : (a + 1) * K] for a in range(4)], axis=0).astype(BF16)
    n_id = iota((FRAMES, FRAMES), 0)
    at = lax.rem(n_id, 64) // 4 * FR + n_id // 64 * 4 + lax.rem(n_id, 4)
    order = jnp.where(at == iota((FRAMES, FRAMES), 1), 1.0, 0.0).astype(BF16)
    om = mm_tn(om, order)
    orders[0] = order
    orders[1] = mm(order, low).astype(BF16)
    probe = om - mm(om.astype(BF16), low)
    probe2 = stacked(probe, 2)

    def block_wait(k):
        source = lax.rem(me + N_TM - k, N_TM)
        pltpu.make_async_remote_copy(
            src_ref=out_buf.at[k], dst_ref=seen.at[:, rows_at(source), :],
            send_sem=s_s.at[source], recv_sem=s_r.at[source], device_id=(tile, source), device_id_type=MESH,
        ).wait_recv()

    for copy in c_copies:
        copy.wait_recv()
    rims_in = fix[...].reshape(len(EARLY) * SHARE, 2 * W)
    for g in range(FR // 2):
        share[:, 2 * g * W : 2 * (g + 1) * W] = mm(rims_in, rim_matrix(g))
    for i, k in enumerate(EARLY):
        block_wait(k)
        window = rows_at(lax.rem(me + N_TM - k, N_TM))
        moved = rows_of(share[i * SHARE : (i + 1) * SHARE, :], i % 2)
        seen[:, window, :] = (seen[:, window, :].astype(F32) - moved).astype(BF16)
    for k in far_first:
        if k not in EARLY:
            block_wait(k)

    def pair(i):
        return jnp.concatenate([seen[2 * i], seen[2 * i + 1]], axis=1)

    for i in range(SHARE // 2):
        y_buf[:, i * 256 : (i + 1) * 256] = stacked(fold(mm(probe2, pair(i)), 2), 2)
    pack_gram(g_mine, gram(y_buf[...]))
    x_copies = []

    def to_half(src, dst, ss, rs):
        dst[place] = src[...]
        for k in (4, 3, 5, 2, 6, 1, 7):
            other = lax.rem(place + k, HALF)
            copy = pltpu.make_async_remote_copy(
                src_ref=src, dst_ref=dst.at[place], send_sem=ss.at[other], recv_sem=rs.at[place],
                device_id=(tile, half * HALF + other), device_id_type=MESH,
            )
            copy.start()
            x_copies.append(copy)

    def from_half(src, dst, ss, rs):
        for k in range(1, HALF):
            other = lax.rem(place + k, HALF)
            pltpu.make_async_remote_copy(
                src_ref=src, dst_ref=dst.at[other], send_sem=ss.at[other], recv_sem=rs.at[other],
                device_id=(tile, half * HALF + other), device_id_type=MESH,
            ).wait_recv()

    to_half(g_mine, g_slots, g_s, g_r)
    back = jnp.zeros((2 * K, FRAMES), F32)
    for i in range(SHARE // 2):
        back = back + mm_nt(y_buf[:, i * 256 : (i + 1) * 256], pair(i))
    b_mine[...] = fold(back, 2).astype(BF16)
    to_half(b_mine, b_slots, b_s, b_r)
    from_half(g_mine, g_slots, g_s, g_r)
    g_sum = g_slots[0]
    for i in range(1, HALF):
        g_sum = g_sum + g_slots[i]
    first = inverse_factors([unpack_gram(g_sum)])[0]
    from_half(b_mine, b_slots, b_s, b_r)
    b_sum = b_slots[0].astype(F32)
    for i in range(1, HALF):
        b_sum = b_sum + b_slots[i].astype(F32)

    back = b_sum - fold(mm_nt(stacked(b_sum, 3), low), 3)
    loadings = mm(first, back, precision=HIGHEST).astype(BF16)
    probe2 = stacked(loadings.astype(F32) - mm(loadings, low), 2)
    for i in range(SHARE // 2):
        r = fold(mm(probe2, pair(i)), 2)
        r_buf[:, i * 256 : (i + 1) * 256] = r
        y_buf[:, i * 256 : (i + 1) * 256] = stacked(r, 2)
    pack_gram(h_mine, gram(y_buf[...]))

    own_first = [half * HALF + lax.rem(place + k, HALF) for k in (4, 3, 5, 2, 6, 1, 7)]
    own_first += [(1 - half) * HALF + lax.rem(place + k, HALF) for k in (0, 1, 7, 2, 6, 3, 5, 4)]

    def to_all(peers, src, dst, ss, rs):
        for peer in peers:
            copy = pltpu.make_async_remote_copy(
                src_ref=src(peer), dst_ref=dst.at[me], send_sem=ss.at[peer], recv_sem=rs.at[me],
                device_id=(tile, peer), device_id_type=MESH,
            )
            copy.start()
            x_copies.append(copy)

    def from_all(sources, src, dst, ss, rs):
        for source in sources:
            pltpu.make_async_remote_copy(
                src_ref=src(source), dst_ref=dst.at[source], send_sem=ss.at[source], recv_sem=rs.at[source],
                device_id=(tile, source), device_id_type=MESH,
            ).wait_recv()

    to_all(own_first[7:] + own_first[:7], lambda peer: h_mine, h_slots, h_s, h_r)
    h_slots[me] = h_mine[...]
    down_p = jnp.zeros((2 * K, FRAMES), F32)
    for i in range(SHARE // 2):
        down_p = down_p + mm_nt(y_buf[:, i * 256 : (i + 1) * 256], pair(i))
    moved = stacked(fold(down_p, 2), 2)
    moved = fold_lanes(mm_nt(orders[0], moved) - mm_nt(orders[1], moved), 2)
    moved = jnp.concatenate([moved[64 * a : 64 * a + 64] for a in range(4)], axis=1)
    d_mine[...] = moved.reshape(N_TM, 4, 4 * K).astype(BF16)
    to_all([lax.rem(me + k, N_TM) for k in far_first], lambda peer: d_mine.at[peer], d_slots, d_s, d_r)
    d_slots[me] = d_mine[me]

    def factor_of(side):
        total = h_slots[side * HALF]
        for i in range(1, HALF):
            total = total + h_slots[side * HALF + i]
        return inverse_factors([unpack_gram(total)])[0]

    def coefficients(side, factor):
        total = d_slots[side * HALF].astype(F32)
        for i in range(1, HALF):
            total = total + d_slots[side * HALF + i].astype(F32)
        coef_ref[side] = mm_nt(unpack_rows(total), factor, precision=HIGHEST)

    other = 1 - half
    from_all(own_first[:7], lambda peer: h_mine, h_slots, h_s, h_r)
    own = factor_of(half)
    final = own * math.sqrt(ROWS // 2 * W)
    for i in range(SHARE // 2):
        two = mm(final, r_buf[:, i * 256 : (i + 1) * 256], precision=HIGHEST)
        for j in range(2):
            basis_ref[pl.ds(2 * i + j, K, stride=SHARE), :] = two[:, j * W : (j + 1) * W]
    from_all(own_first[7:], lambda peer: h_mine, h_slots, h_s, h_r)
    distant = factor_of(other)
    from_all(own_first, lambda peer: d_mine.at[peer], d_slots, d_s, d_r)
    coefficients(half, own)
    coefficients(other, distant)

    for copy in halo:
        copy.wait_send()
    for copy in om_copies + s_copies + c_copies:
        copy.wait_send()
    for copy in x_copies:
        copy.wait_send()


def write_out(basis, coef, basis_out, coef_out, sems):
    copies = [pltpu.make_async_copy(basis, basis_out, sems.at[0]), pltpu.make_async_copy(coef, coef_out, sems.at[1])]
    for copy in copies:
        copy.start()
    for copy in copies:
        copy.wait()


def solution(mesh):
    n_tile = mesh.shape["tile"]

    def local(movie, omega, time_taps, space_taps):
        dma = pltpu.SemaphoreType.DMA
        vmem = pl.BlockSpec(memory_space=pltpu.VMEM)
        basis, coef = pl.pallas_call(
            functools.partial(kernel, n_tile),
            out_shape=(
                pltpu.VMEM((K * SHARE, W), F32),
                pltpu.VMEM((2, FR, K), F32),
            ),
            in_specs=[pl.BlockSpec(memory_space=pl.ANY)] * 4,
            out_specs=(vmem, vmem),
            scratch_shapes=[
                pltpu.VMEM((FR, ROWS, W), BF16),
                pltpu.VMEM((2, FR, K), BF16),
                pltpu.VMEM((2, 4, 4 * K), BF16),
                pltpu.VMEM((len(EARLY), SHARE, 2 * W), BF16),
                pltpu.VMEM((ROWS, 2 * W), BF16),
                pltpu.VMEM((len(EARLY) * SHARE, FR * W), F32),
                pltpu.VMEM((1, 2 * RAD + 1), BF16),
                pltpu.VMEM((1, 2 * RAD + 1), BF16),
                pltpu.VMEM((ROWS, FR * W), F32),
                pltpu.VMEM((2, ROWS, W), BF16),
                pltpu.VMEM((2, ROWS, W), BF16),
                pltpu.VMEM((2, SHARE * FR, W), F32),
                pltpu.VMEM((N_TM, SHARE, FR, W), BF16),
                pltpu.VMEM((SHARE, FRAMES, W), BF16),
                pltpu.VMEM((N_TM, 4, 4 * K), BF16),
                pltpu.VMEM((HALF, K, FRAMES), BF16),
                pltpu.VMEM((HALF, 8, 128), F32),
                pltpu.VMEM((K, FRAMES), BF16),
                pltpu.VMEM((8, 128), F32),
                pltpu.VMEM((2, FRAMES, FRAMES), BF16),
                pltpu.VMEM((8, 128), F32),
                pltpu.VMEM((N_TM, 8, 128), F32),
                pltpu.VMEM((N_TM, 4, 4 * K), BF16),
                pltpu.VMEM((N_TM, 4, 4 * K), BF16),
                pltpu.VMEM((2 * K, PIX), BF16),
                pltpu.VMEM((K, PIX), F32),
                dma((4,)), dma((2,)), dma((2,)), dma((N_TM,)), dma((N_TM,)), dma((N_TM,)), dma((N_TM,)),
                dma((len(EARLY),)), dma((len(EARLY),)),
                dma((HALF,)), dma((HALF,)), dma((HALF,)), dma((HALF,)),
                dma((N_TM,)), dma((N_TM,)), dma((N_TM,)), dma((N_TM,)),
            ],
            compiler_params=pltpu.CompilerParams(collective_id=0, has_side_effects=True),
            name="low_rank",
        )(
            movie,
            jnp.transpose(omega[:, 0], (0, 2, 1)),
            time_taps.reshape(1, -1),
            space_taps.reshape(1, -1),
        )
        basis, coef = pl.pallas_call(
            write_out,
            out_shape=(
                jax.ShapeDtypeStruct((K * SHARE, W), F32),
                jax.ShapeDtypeStruct((2, FR, K), F32),
            ),
            in_specs=[pl.BlockSpec(memory_space=pltpu.VMEM)] * 2,
            out_specs=(pl.BlockSpec(memory_space=pl.ANY),) * 2,
            scratch_shapes=[dma((2,))],
            name="write_out",
        )(pltpu.with_memory_space_constraint(basis, pltpu.VMEM), pltpu.with_memory_space_constraint(coef, pltpu.VMEM))
        return basis.reshape(K, SHARE, W), jnp.transpose(coef, (0, 2, 1))[:, None]

    in_specs = (P("tm", None, "tile"), P(None, "tile", None, "tm"), P(), P())
    out_specs = (P(None, "tm", "tile"), P(None, "tile", None, "tm"))
    return jax.shard_map(local, mesh=mesh, in_specs=in_specs, out_specs=out_specs, check_vma=False)
```

```python
import functools
import math

import jax
import jax.numpy as jnp
from jax import lax
from jax.experimental import pallas as pl
from jax.experimental.pallas import tpu as pltpu
from jax.sharding import PartitionSpec as P

MESH = pl.DeviceIdType.MESH
F32 = jnp.float32
BF16 = jnp.bfloat16
HIGHEST = lax.Precision.HIGHEST

N_TM = 16
HALF = 8
FR = 16
FRAMES = 256
ROWS = 256
SHARE = 16
W = 128
K = 32
RAD = 8
PIX = SHARE * W
EARLY = 2


def mm(a, b, **kw):
    return jnp.dot(a, b, preferred_element_type=F32, **kw)


def mm_nt(a, b, **kw):
    return lax.dot_general(a, b, (((1,), (1,)), ((), ())), preferred_element_type=F32, **kw)


def mm_tn(a, b, **kw):
    return lax.dot_general(a, b, (((0,), (0,)), ((), ())), preferred_element_type=F32, **kw)


def pieces(x, count):
    out = []
    for _ in range(count - 1):
        part = x.astype(BF16)
        out.append(part)
        x = x - part.astype(F32)
    out.append(x.astype(BF16))
    return out


def stacked(x, count, axis=0):
    return jnp.concatenate(pieces(x, count), axis=axis)


def fold(x, count):
    total = x[:K]
    for i in range(1, count):
        total = total + x[i * K : (i + 1) * K]
    return total


def fold_lanes(x, count):
    total = x[:, :K]
    for i in range(1, count):
        total = total + x[:, i * K : (i + 1) * K]
    return total


def iota(shape, dim):
    return lax.broadcasted_iota(jnp.int32, shape, dim)


def from_taps(taps, index):
    out = jnp.zeros(index.shape, F32)
    for k in range(2 * RAD + 1):
        out = jnp.where(index == k, taps[:, k : k + 1], out)
    return out


def gram(x2):
    return fold_lanes(fold(mm_nt(x2, x2), 2), 2)


def inverse_factors(grams):
    row = iota((8, 128), 0)
    eye = jnp.where(iota((K, K), 0) == iota((K, K), 1), 1.0, 0.0)
    state = []
    for g in grams:
        aug = jnp.concatenate([g, eye, jnp.zeros((K, 64), F32)], axis=1)
        state.append(([aug[8 * i : 8 * i + 8] for i in range(4)], []))
    for b in range(4):
        spread = [
            [[jnp.broadcast_to(aug[i][:, 8 * b + t : 8 * b + t + 1], (8, 128)) for i in range(b, 4)] for t in range(8)]
            for aug, _ in state
        ]
        scale = [jnp.ones((8, 128), F32) for _ in state]
        for t in range(8):
            for n, (aug, _) in enumerate(state):
                cols = spread[n]
                pivot = cols[t][0][t : t + 1, :]
                inverse = 1.0 / pivot
                scale[n] = jnp.where(row == t, pivot, scale[n])
                line = aug[b][t : t + 1, :] * inverse
                heads = [cols[u][0][t : t + 1, :] * inverse for u in range(t + 1, 8)]
                for i in range(b, 4):
                    factor = cols[t][i - b]
                    if i == b:
                        factor = jnp.where(row > t, factor, 0.0)
                    aug[i] = aug[i] - factor * line
                    for u in range(t + 1, 8):
                        cols[u][i - b] = cols[u][i - b] - factor * heads[u - t - 1]
        for n, (aug, done) in enumerate(state):
            done.append(aug[b] * lax.rsqrt(scale[n]))
    return [jnp.concatenate(done, axis=0)[:, K : 2 * K] for _, done in state]


def toeplitz(taps, size, flip):
    lane, row = iota((8, size), 1), iota((8, size), 0)
    head = from_taps(taps, row + 2 * RAD - lane if flip else lane - row)
    rows = []
    for i in range(size // 8):
        block = head
        if i == 0:
            block = jnp.where(lane >= 8, head, 0.0)
        if i == size // 8 - 1:
            block = jnp.where(lane < 16, head, 0.0)
        shift = (8 * i - 8) % size
        rows.append(pltpu.roll(block, shift, 1) if shift else block)
    return jnp.concatenate(rows, axis=0).astype(BF16)


def zeros16(*shape):
    return jnp.zeros(shape, BF16)


def pack_gram(ref, g):
    for i in range(4):
        ref[:, i * K : (i + 1) * K] = g[8 * i : 8 * i + 8, :]


def unpack_rows(total):
    return jnp.concatenate([total[:, i * K : (i + 1) * K] for i in range(4)], axis=0)


def unpack_gram(total):
    return jnp.concatenate([total[:, i * K : (i + 1) * K] for i in range(4)], axis=0)


def kernel(
    n_tile,
    movie_hbm, omega_hbm, time_hbm, space_hbm,
    basis_ref, coef_ref,
    movie, omega_ref, om_mine, fix, rim_buf, share, time_ref, space_ref, far, packed, edge, turn, out_buf, seen, om_all,
    b_slots, g_slots, b_mine, g_mine, orders, h_mine, h_slots, d_mine, d_slots, y_buf, r_buf,
    load_sem, halo_s, halo_r, s_s, s_r, om_s, om_r, c_s, c_r, b_s, b_r, g_s, g_r, h_s, h_r, d_s, d_r,
):
    tile = lax.axis_index("tile")
    me = lax.axis_index("tm")
    half = me // HALF
    place = me - half * HALF
    left = lax.rem(tile + n_tile - 1, n_tile)
    right = lax.rem(tile + 1, n_tile)
    far_first = (8, 7, 9, 6, 10, 5, 11, 4, 12, 3, 13, 2, 14, 1, 15)
    core = lax.rem(me, 2)
    send_order = (8, 7 + 2 * core, 9 - 2 * core) + far_first[3:]
    recv_order = (8, 9 - 2 * core, 7 + 2 * core) + far_first[3:]

    loads = [
        pltpu.make_async_copy(src, dst, load_sem.at[i])
        for i, (src, dst) in enumerate(
            ((movie_hbm, movie), (space_hbm, space_ref), (time_hbm, time_ref), (omega_hbm, omega_ref))
        )
    ]
    for load in loads:
        load.start()
    barrier = pltpu.get_barrier_semaphore()
    for k in far_first:
        pl.semaphore_signal(barrier, inc=1, device_id=(tile, lax.rem(me + k, N_TM)), device_id_type=MESH)
    pl.semaphore_signal(barrier, inc=1, device_id=(left, me), device_id_type=MESH)
    pl.semaphore_signal(barrier, inc=1, device_id=(right, me), device_id_type=MESH)

    loads[1].wait()
    space = space_ref[...].astype(F32)
    down = toeplitz(space, ROWS, False)
    side = toeplitz(space, W, True)
    across = jnp.concatenate(
        [jnp.concatenate([side, zeros16(W, W)], axis=1), jnp.concatenate([zeros16(W, W), side], axis=1)], axis=0
    )
    lane8, row8 = iota((8, W), 1), iota((8, W), 0)
    none8 = jnp.zeros((8, W), F32)
    rims = []
    for offset in (136, 0):
        one = from_taps(space, offset + row8 - lane8)
        rims.append(
            jnp.concatenate(
                [jnp.concatenate([one, none8], axis=1), jnp.concatenate([none8, one], axis=1)], axis=0
            ).astype(BF16)
        )
    unit = jnp.where(lane8 == row8, 1.0, 0.0)
    picks = []
    for f in range(FR):
        moved = pltpu.roll(unit, 8 * f, 1) if f else unit
        top = jnp.concatenate([moved, none8], axis=0).astype(BF16)
        bottom = jnp.concatenate([none8, moved], axis=0).astype(BF16)
        picks.append(jnp.concatenate([top, zeros16(16, W)], axis=1))
        picks.append(zeros16(W - 32, 2 * W))
        picks.append(jnp.concatenate([zeros16(16, W), bottom], axis=1))
    loads[0].wait()

    def frames2(g):
        return jnp.concatenate([movie[2 * g], movie[2 * g + 1]], axis=1)

    total = mm(jnp.concatenate([movie[f] for f in range(FR)], axis=1), jnp.concatenate(picks, axis=0))
    packed[0] = total[:, :W].astype(BF16)
    packed[1] = total[:, W:].astype(BF16)

    for g in range(FR // 2):
        two = frames2(g)
        mid = mm(down, two).astype(BF16)
        far[:, 2 * g * W : 2 * (g + 1) * W] = two.astype(F32) - mm(mid, across)


    def rows_of(values, slot):
        for f in range(FR):
            turn[slot, pl.ds(f, SHARE, stride=FR), :] = values[:, f * W : (f + 1) * W]
        return turn[slot].reshape(SHARE, FR, W)

    def rows_at(peer):
        return pl.ds(pl.multiple_of(peer * SHARE, SHARE), SHARE)

    s_copies = []

    def block_copy(i):
        peer = lax.rem(me + send_order[i], N_TM)
        return pltpu.make_async_remote_copy(
            src_ref=out_buf.at[i], dst_ref=seen.at[:, rows_at(me), :],
            send_sem=s_s.at[peer], recv_sem=s_r.at[me], device_id=(tile, peer), device_id_type=MESH,
        )

    for i in range(EARLY):
        out_buf[i] = rows_of(far[rows_at(lax.rem(me + send_order[i], N_TM)), :], i % 2).astype(BF16)
    loads[2].wait()
    loads[3].wait()
    for i in range(2):
        some = omega_ref[i].astype(F32)
        om_mine[i] = jnp.concatenate([some[4 * a : 4 * a + 4] for a in range(4)], axis=1).astype(BF16)

    pl.semaphore_wait(barrier, N_TM - 1 + 2)
    halo = []
    for i, target in ((0, left), (1, right)):
        copy = pltpu.make_async_remote_copy(
            src_ref=packed.at[i], dst_ref=edge.at[i], send_sem=halo_s.at[i], recv_sem=halo_r.at[i],
            device_id=(target, me), device_id_type=MESH,
        )
        copy.start()
        halo.append(copy)
    for i in range(EARLY):
        s_copies.append(block_copy(i))
        s_copies[-1].start()
    om_copies = []
    for k in far_first:
        peer = lax.rem(me + k, N_TM)
        copy = pltpu.make_async_remote_copy(
            src_ref=om_mine.at[peer // HALF], dst_ref=om_all.at[me],
            send_sem=om_s.at[peer], recv_sem=om_r.at[me], device_id=(tile, peer), device_id_type=MESH,
        )
        copy.start()
        om_copies.append(copy)
    om_all[me] = om_mine[half]

    for i in range(2):
        halo[i].wait_recv()
    rim_right = jnp.where(tile < n_tile - 1, edge[0].astype(F32), 0.0).astype(BF16)
    rim_left = jnp.where(tile > 0, edge[1].astype(F32), 0.0).astype(BF16)
    rim = mm(down, jnp.concatenate([rim_right, rim_left], axis=1)).astype(BF16)
    rim_buf[...] = rim
    c_copies = []
    for i in range(EARLY):
        peer = lax.rem(me + send_order[i], N_TM)
        copy = pltpu.make_async_remote_copy(
            src_ref=rim_buf.at[rows_at(peer), :], dst_ref=fix.at[i],
            send_sem=c_s.at[i], recv_sem=c_r.at[i], device_id=(tile, peer), device_id_type=MESH,
        )
        copy.start()
        c_copies.append(copy)

    def rim_matrix(g):
        rows = []
        for i in range(2):
            rows += [zeros16(16 * g, 2 * W)] if g else []
            rows += [rims[i]]
            rows += [zeros16(W - 16 * g - 16, 2 * W)] if g < FR // 2 - 1 else []
        return jnp.concatenate(rows, axis=0)

    for g in range(FR // 2):
        window = slice(2 * g * W, 2 * (g + 1) * W)
        far[:, window] = far[:, window] - mm(rim, rim_matrix(g))

    for i in range(EARLY, N_TM - 1):
        out_buf[i] = rows_of(far[rows_at(lax.rem(me + send_order[i], N_TM)), :], i % 2).astype(BF16)
        s_copies.append(block_copy(i))
        s_copies[-1].start()
    seen[:, rows_at(me), :] = rows_of(far[rows_at(me), :], 1).astype(BF16)

    time = time_ref[...].astype(F32)
    low = toeplitz(time, FRAMES, False)
    for k in range(1, N_TM):
        source = lax.rem(me + k, N_TM)
        pltpu.make_async_remote_copy(
            src_ref=om_mine.at[0], dst_ref=om_all.at[source], send_sem=om_s.at[source], recv_sem=om_r.at[source],
            device_id=(tile, source), device_id_type=MESH,
        ).wait_recv()
    om = om_all[...].astype(F32).reshape(4 * N_TM, 128)
    om = jnp.concatenate([om[:, a * K : (a + 1) * K] for a in range(4)], axis=0).astype(BF16)
    n_id = iota((FRAMES, FRAMES), 0)
    at = lax.rem(n_id, 64) // 4 * FR + n_id // 64 * 4 + lax.rem(n_id, 4)
    order = jnp.where(at == iota((FRAMES, FRAMES), 1), 1.0, 0.0).astype(BF16)
    om = mm_tn(om, order)
    orders[0] = order
    orders[1] = mm(order, low).astype(BF16)
    probe = om - mm(om.astype(BF16), low)
    probe2 = stacked(probe, 2)

    def block_wait(i):
        source = lax.rem(me + N_TM - recv_order[i], N_TM)
        pltpu.make_async_remote_copy(
            src_ref=out_buf.at[i], dst_ref=seen.at[:, rows_at(source), :],
            send_sem=s_s.at[source], recv_sem=s_r.at[source], device_id=(tile, source), device_id_type=MESH,
        ).wait_recv()

    for copy in c_copies:
        copy.wait_recv()
    rims_in = fix[...].reshape(EARLY * SHARE, 2 * W)
    for g in range(FR // 2):
        share[:, 2 * g * W : 2 * (g + 1) * W] = mm(rims_in, rim_matrix(g))
    for i in range(EARLY):
        block_wait(i)
        window = rows_at(lax.rem(me + N_TM - recv_order[i], N_TM))
        moved = rows_of(share[i * SHARE : (i + 1) * SHARE, :], i % 2)
        seen[:, window, :] = (seen[:, window, :].astype(F32) - moved).astype(BF16)
    for i in range(EARLY, N_TM - 1):
        block_wait(i)

    def pair(i):
        return jnp.concatenate([seen[2 * i], seen[2 * i + 1]], axis=1)

    for i in range(SHARE // 2):
        y_buf[:, i * 256 : (i + 1) * 256] = stacked(fold(mm(probe2, pair(i)), 2), 2)
    pack_gram(g_mine, gram(y_buf[...]))
    x_copies = []

    def to_half(src, dst, ss, rs):
        dst[place] = src[...]
        for k in (4, 3, 5, 2, 6, 1, 7):
            other = lax.rem(place + k, HALF)
            copy = pltpu.make_async_remote_copy(
                src_ref=src, dst_ref=dst.at[place], send_sem=ss.at[other], recv_sem=rs.at[place],
                device_id=(tile, half * HALF + other), device_id_type=MESH,
            )
            copy.start()
            x_copies.append(copy)

    def from_half(src, dst, ss, rs):
        for k in range(1, HALF):
            other = lax.rem(place + k, HALF)
            pltpu.make_async_remote_copy(
                src_ref=src, dst_ref=dst.at[other], send_sem=ss.at[other], recv_sem=rs.at[other],
                device_id=(tile, half * HALF + other), device_id_type=MESH,
            ).wait_recv()

    to_half(g_mine, g_slots, g_s, g_r)
    back = jnp.zeros((2 * K, FRAMES), F32)
    for i in range(SHARE // 2):
        back = back + mm_nt(y_buf[:, i * 256 : (i + 1) * 256], pair(i))
    b_mine[...] = fold(back, 2).astype(BF16)
    to_half(b_mine, b_slots, b_s, b_r)
    from_half(g_mine, g_slots, g_s, g_r)
    g_sum = g_slots[0]
    for i in range(1, HALF):
        g_sum = g_sum + g_slots[i]
    first = inverse_factors([unpack_gram(g_sum)])[0]
    from_half(b_mine, b_slots, b_s, b_r)
    b_sum = b_slots[0].astype(F32)
    for i in range(1, HALF):
        b_sum = b_sum + b_slots[i].astype(F32)

    back = b_sum - fold(mm_nt(stacked(b_sum, 3), low), 3)
    loadings = mm(first, back, precision=HIGHEST).astype(BF16)
    probe2 = stacked(loadings.astype(F32) - mm(loadings, low), 2)
    for i in range(SHARE // 2):
        r = fold(mm(probe2, pair(i)), 2)
        r_buf[:, i * 256 : (i + 1) * 256] = r
        y_buf[:, i * 256 : (i + 1) * 256] = stacked(r, 2)
    pack_gram(h_mine, gram(y_buf[...]))

    own_first = [half * HALF + lax.rem(place + k, HALF) for k in (4, 3, 5, 2, 6, 1, 7)]
    own_first += [(1 - half) * HALF + lax.rem(place + k, HALF) for k in (0, 1, 7, 2, 6, 3, 5, 4)]

    def to_all(peers, src, dst, ss, rs):
        for peer in peers:
            copy = pltpu.make_async_remote_copy(
                src_ref=src(peer), dst_ref=dst.at[me], send_sem=ss.at[peer], recv_sem=rs.at[me],
                device_id=(tile, peer), device_id_type=MESH,
            )
            copy.start()
            x_copies.append(copy)

    def from_all(sources, src, dst, ss, rs):
        for source in sources:
            pltpu.make_async_remote_copy(
                src_ref=src(source), dst_ref=dst.at[source], send_sem=ss.at[source], recv_sem=rs.at[source],
                device_id=(tile, source), device_id_type=MESH,
            ).wait_recv()

    to_all(own_first[7:] + own_first[:7], lambda peer: h_mine, h_slots, h_s, h_r)
    h_slots[me] = h_mine[...]
    down_p = jnp.zeros((2 * K, FRAMES), F32)
    for i in range(SHARE // 2):
        down_p = down_p + mm_nt(y_buf[:, i * 256 : (i + 1) * 256], pair(i))
    moved = stacked(fold(down_p, 2), 2)
    moved = fold_lanes(mm_nt(orders[0], moved) - mm_nt(orders[1], moved), 2)
    moved = jnp.concatenate([moved[64 * a : 64 * a + 64] for a in range(4)], axis=1)
    d_mine[...] = moved.reshape(N_TM, 4, 4 * K).astype(BF16)
    to_all([lax.rem(me + k, N_TM) for k in far_first], lambda peer: d_mine.at[peer], d_slots, d_s, d_r)
    d_slots[me] = d_mine[me]

    def factor_of(side):
        total = h_slots[side * HALF]
        for i in range(1, HALF):
            total = total + h_slots[side * HALF + i]
        return inverse_factors([unpack_gram(total)])[0]

    def coefficients(side, factor):
        total = d_slots[side * HALF].astype(F32)
        for i in range(1, HALF):
            total = total + d_slots[side * HALF + i].astype(F32)
        coef_ref[side] = mm_nt(unpack_rows(total), factor, precision=HIGHEST)

    other = 1 - half
    from_all(own_first[:7], lambda peer: h_mine, h_slots, h_s, h_r)
    own = factor_of(half)
    final = own * math.sqrt(ROWS // 2 * W)
    for i in range(SHARE // 2):
        two = mm(final, r_buf[:, i * 256 : (i + 1) * 256], precision=HIGHEST)
        for j in range(2):
            basis_ref[pl.ds(2 * i + j, K, stride=SHARE), :] = two[:, j * W : (j + 1) * W]
    from_all(own_first[7:], lambda peer: h_mine, h_slots, h_s, h_r)
    distant = factor_of(other)
    from_all(own_first, lambda peer: d_mine.at[peer], d_slots, d_s, d_r)
    coefficients(half, own)
    coefficients(other, distant)

    for copy in halo:
        copy.wait_send()
    for copy in om_copies + s_copies + c_copies:
        copy.wait_send()
    for copy in x_copies:
        copy.wait_send()


def write_out(basis, coef, basis_out, coef_out, sems):
    copies = [pltpu.make_async_copy(basis, basis_out, sems.at[0]), pltpu.make_async_copy(coef, coef_out, sems.at[1])]
    for copy in copies:
        copy.start()
    for copy in copies:
        copy.wait()


def solution(mesh):
    n_tile = mesh.shape["tile"]

    def local(movie, omega, time_taps, space_taps):
        dma = pltpu.SemaphoreType.DMA
        vmem = pl.BlockSpec(memory_space=pltpu.VMEM)
        basis, coef = pl.pallas_call(
            functools.partial(kernel, n_tile),
            out_shape=(
                pltpu.VMEM((K * SHARE, W), F32),
                pltpu.VMEM((2, FR, K), F32),
            ),
            in_specs=[pl.BlockSpec(memory_space=pl.ANY)] * 4,
            out_specs=(vmem, vmem),
            scratch_shapes=[
                pltpu.VMEM((FR, ROWS, W), BF16),
                pltpu.VMEM((2, FR, K), BF16),
                pltpu.VMEM((2, 4, 4 * K), BF16),
                pltpu.VMEM((EARLY, SHARE, 2 * W), BF16),
                pltpu.VMEM((ROWS, 2 * W), BF16),
                pltpu.VMEM((EARLY * SHARE, FR * W), F32),
                pltpu.VMEM((1, 2 * RAD + 1), BF16),
                pltpu.VMEM((1, 2 * RAD + 1), BF16),
                pltpu.VMEM((ROWS, FR * W), F32),
                pltpu.VMEM((2, ROWS, W), BF16),
                pltpu.VMEM((2, ROWS, W), BF16),
                pltpu.VMEM((2, SHARE * FR, W), F32),
                pltpu.VMEM((N_TM, SHARE, FR, W), BF16),
                pltpu.VMEM((SHARE, FRAMES, W), BF16),
                pltpu.VMEM((N_TM, 4, 4 * K), BF16),
                pltpu.VMEM((HALF, K, FRAMES), BF16),
                pltpu.VMEM((HALF, 8, 128), F32),
                pltpu.VMEM((K, FRAMES), BF16),
                pltpu.VMEM((8, 128), F32),
                pltpu.VMEM((2, FRAMES, FRAMES), BF16),
                pltpu.VMEM((8, 128), F32),
                pltpu.VMEM((N_TM, 8, 128), F32),
                pltpu.VMEM((N_TM, 4, 4 * K), BF16),
                pltpu.VMEM((N_TM, 4, 4 * K), BF16),
                pltpu.VMEM((2 * K, PIX), BF16),
                pltpu.VMEM((K, PIX), F32),
                dma((4,)), dma((2,)), dma((2,)), dma((N_TM,)), dma((N_TM,)), dma((N_TM,)), dma((N_TM,)),
                dma((EARLY,)), dma((EARLY,)),
                dma((HALF,)), dma((HALF,)), dma((HALF,)), dma((HALF,)),
                dma((N_TM,)), dma((N_TM,)), dma((N_TM,)), dma((N_TM,)),
            ],
            compiler_params=pltpu.CompilerParams(collective_id=0, has_side_effects=True),
            name="low_rank",
        )(
            movie,
            jnp.transpose(omega[:, 0], (0, 2, 1)),
            time_taps.reshape(1, -1),
            space_taps.reshape(1, -1),
        )
        basis, coef = pl.pallas_call(
            write_out,
            out_shape=(
                jax.ShapeDtypeStruct((K * SHARE, W), F32),
                jax.ShapeDtypeStruct((2, FR, K), F32),
            ),
            in_specs=[pl.BlockSpec(memory_space=pltpu.VMEM)] * 2,
            out_specs=(pl.BlockSpec(memory_space=pl.ANY),) * 2,
            scratch_shapes=[dma((2,))],
            name="write_out",
        )(pltpu.with_memory_space_constraint(basis, pltpu.VMEM), pltpu.with_memory_space_constraint(coef, pltpu.VMEM))
        return basis.reshape(K, SHARE, W), jnp.transpose(coef, (0, 2, 1))[:, None]

    in_specs = (P("tm", None, "tile"), P(None, "tile", None, "tm"), P(), P())
    out_specs = (P(None, "tm", "tile"), P(None, "tile", None, "tm"))
    return jax.shard_map(local, mesh=mesh, in_specs=in_specs, out_specs=out_specs, check_vma=False)
```

```python
import functools
import math

import jax
import jax.numpy as jnp
from jax import lax
from jax.experimental import pallas as pl
from jax.experimental.pallas import tpu as pltpu
from jax.sharding import PartitionSpec as P

MESH = pl.DeviceIdType.MESH
F32 = jnp.float32
BF16 = jnp.bfloat16
HIGHEST = lax.Precision.HIGHEST

N_TM = 16
HALF = 8
FR = 16
FRAMES = 256
ROWS = 256
SHARE = 16
W = 128
K = 32
RAD = 8
PIX = SHARE * W
EARLY = 2


def mm(a, b, **kw):
    return jnp.dot(a, b, preferred_element_type=F32, **kw)


def mm_nt(a, b, **kw):
    return lax.dot_general(a, b, (((1,), (1,)), ((), ())), preferred_element_type=F32, **kw)


def mm_tn(a, b, **kw):
    return lax.dot_general(a, b, (((0,), (0,)), ((), ())), preferred_element_type=F32, **kw)


def pieces(x, count):
    out = []
    for _ in range(count - 1):
        part = x.astype(BF16)
        out.append(part)
        x = x - part.astype(F32)
    out.append(x.astype(BF16))
    return out


def stacked(x, count, axis=0):
    return jnp.concatenate(pieces(x, count), axis=axis)


def fold(x, count):
    total = x[:K]
    for i in range(1, count):
        total = total + x[i * K : (i + 1) * K]
    return total


def fold_lanes(x, count):
    total = x[:, :K]
    for i in range(1, count):
        total = total + x[:, i * K : (i + 1) * K]
    return total


def iota(shape, dim):
    return lax.broadcasted_iota(jnp.int32, shape, dim)


def from_taps(taps, index):
    out = jnp.zeros(index.shape, F32)
    for k in range(2 * RAD + 1):
        out = jnp.where(index == k, taps[:, k : k + 1], out)
    return out


def gram(x2):
    return fold_lanes(fold(mm_nt(x2, x2), 2), 2)


def inverse_factors(grams):
    row = iota((8, 128), 0)
    eye = jnp.where(iota((K, K), 0) == iota((K, K), 1), 1.0, 0.0)
    state = []
    for g in grams:
        aug = jnp.concatenate([g, eye, jnp.zeros((K, 64), F32)], axis=1)
        state.append(([aug[8 * i : 8 * i + 8] for i in range(4)], []))
    for b in range(4):
        spread = [
            [[jnp.broadcast_to(aug[i][:, 8 * b + t : 8 * b + t + 1], (8, 128)) for i in range(b, 4)] for t in range(8)]
            for aug, _ in state
        ]
        scale = [jnp.ones((8, 128), F32) for _ in state]
        for t in range(8):
            for n, (aug, _) in enumerate(state):
                cols = spread[n]
                pivot = cols[t][0][t : t + 1, :]
                inverse = 1.0 / pivot
                scale[n] = jnp.where(row == t, pivot, scale[n])
                line = aug[b][t : t + 1, :] * inverse
                heads = [cols[u][0][t : t + 1, :] * inverse for u in range(t + 1, 8)]
                for i in range(b, 4):
                    factor = cols[t][i - b]
                    if i == b:
                        factor = jnp.where(row > t, factor, 0.0)
                    aug[i] = aug[i] - factor * line
                    for u in range(t + 1, 8):
                        cols[u][i - b] = cols[u][i - b] - factor * heads[u - t - 1]
        for n, (aug, done) in enumerate(state):
            done.append(aug[b] * lax.rsqrt(scale[n]))
    return [jnp.concatenate(done, axis=0)[:, K : 2 * K] for _, done in state]


def toeplitz(taps, size, flip):
    lane, row = iota((8, size), 1), iota((8, size), 0)
    head = from_taps(taps, row + 2 * RAD - lane if flip else lane - row)
    rows = []
    for i in range(size // 8):
        block = head
        if i == 0:
            block = jnp.where(lane >= 8, head, 0.0)
        if i == size // 8 - 1:
            block = jnp.where(lane < 16, head, 0.0)
        shift = (8 * i - 8) % size
        rows.append(pltpu.roll(block, shift, 1) if shift else block)
    return jnp.concatenate(rows, axis=0).astype(BF16)


def zeros16(*shape):
    return jnp.zeros(shape, BF16)


def pack_gram(ref, g):
    for i in range(4):
        ref[:, i * K : (i + 1) * K] = g[8 * i : 8 * i + 8, :]


def unpack_rows(total):
    return jnp.concatenate([total[:, i * K : (i + 1) * K] for i in range(4)], axis=0)


def unpack_gram(total):
    return jnp.concatenate([total[:, i * K : (i + 1) * K] for i in range(4)], axis=0)


def kernel(
    n_tile,
    movie_hbm, omega_hbm, time_hbm, space_hbm,
    basis_ref, coef_ref,
    movie, omega_ref, om_mine, fix, rim_buf, share, time_ref, space_ref, far, packed, edge, turn, out_buf, seen, om_all,
    b_slots, g_slots, b_mine, g_mine, orders, twice, h_mine, h_slots, d_mine, d_slots, y_buf, r_buf,
    load_sem, halo_s, halo_r, s_s, s_r, om_s, om_r, c_s, c_r, b_s, b_r, g_s, g_r, h_s, h_r, d_s, d_r,
):
    tile = lax.axis_index("tile")
    me = lax.axis_index("tm")
    half = me // HALF
    place = me - half * HALF
    left = lax.rem(tile + n_tile - 1, n_tile)
    right = lax.rem(tile + 1, n_tile)
    far_first = (8, 7, 9, 6, 10, 5, 11, 4, 12, 3, 13, 2, 14, 1, 15)
    core = lax.rem(me, 2)
    send_order = (8, 7 + 2 * core, 9 - 2 * core) + far_first[3:]
    recv_order = (8, 9 - 2 * core, 7 + 2 * core) + far_first[3:]

    loads = [
        pltpu.make_async_copy(src, dst, load_sem.at[i])
        for i, (src, dst) in enumerate(
            ((movie_hbm, movie), (space_hbm, space_ref), (time_hbm, time_ref), (omega_hbm, omega_ref))
        )
    ]
    for load in loads:
        load.start()
    barrier = pltpu.get_barrier_semaphore()
    for k in far_first:
        pl.semaphore_signal(barrier, inc=1, device_id=(tile, lax.rem(me + k, N_TM)), device_id_type=MESH)
    pl.semaphore_signal(barrier, inc=1, device_id=(left, me), device_id_type=MESH)
    pl.semaphore_signal(barrier, inc=1, device_id=(right, me), device_id_type=MESH)

    loads[1].wait()
    space = space_ref[...].astype(F32)
    down = toeplitz(space, ROWS, False)
    side = toeplitz(space, W, True)
    across = jnp.concatenate(
        [jnp.concatenate([side, zeros16(W, W)], axis=1), jnp.concatenate([zeros16(W, W), side], axis=1)], axis=0
    )
    lane8, row8 = iota((8, W), 1), iota((8, W), 0)
    none8 = jnp.zeros((8, W), F32)
    rims = []
    for offset in (136, 0):
        one = from_taps(space, offset + row8 - lane8)
        rims.append(
            jnp.concatenate(
                [jnp.concatenate([one, none8], axis=1), jnp.concatenate([none8, one], axis=1)], axis=0
            ).astype(BF16)
        )
    unit = jnp.where(lane8 == row8, 1.0, 0.0)
    picks = []
    for f in range(FR):
        moved = pltpu.roll(unit, 8 * f, 1) if f else unit
        top = jnp.concatenate([moved, none8], axis=0).astype(BF16)
        bottom = jnp.concatenate([none8, moved], axis=0).astype(BF16)
        picks.append(jnp.concatenate([top, zeros16(16, W)], axis=1))
        picks.append(zeros16(W - 32, 2 * W))
        picks.append(jnp.concatenate([zeros16(16, W), bottom], axis=1))
    loads[0].wait()

    def frames2(g):
        return jnp.concatenate([movie[2 * g], movie[2 * g + 1]], axis=1)

    total = mm(jnp.concatenate([movie[f] for f in range(FR)], axis=1), jnp.concatenate(picks, axis=0))
    packed[0] = total[:, :W].astype(BF16)
    packed[1] = total[:, W:].astype(BF16)

    for g in range(FR // 2):
        two = frames2(g)
        mid = mm(down, two).astype(BF16)
        far[:, 2 * g * W : 2 * (g + 1) * W] = two.astype(F32) - mm(mid, across)


    def rows_of(values, slot):
        for f in range(FR):
            turn[slot, pl.ds(f, SHARE, stride=FR), :] = values[:, f * W : (f + 1) * W]
        return turn[slot].reshape(SHARE, FR, W)

    def rows_at(peer):
        return pl.ds(pl.multiple_of(peer * SHARE, SHARE), SHARE)

    s_copies = []

    def block_copy(i):
        peer = lax.rem(me + send_order[i], N_TM)
        return pltpu.make_async_remote_copy(
            src_ref=out_buf.at[i], dst_ref=seen.at[:, rows_at(me), :],
            send_sem=s_s.at[peer], recv_sem=s_r.at[me], device_id=(tile, peer), device_id_type=MESH,
        )

    for i in range(EARLY):
        out_buf[i] = rows_of(far[rows_at(lax.rem(me + send_order[i], N_TM)), :], i % 2).astype(BF16)
    loads[2].wait()
    loads[3].wait()
    for i in range(2):
        some = omega_ref[i].astype(F32)
        om_mine[i] = jnp.concatenate([some[4 * a : 4 * a + 4] for a in range(4)], axis=1).astype(BF16)

    pl.semaphore_wait(barrier, N_TM - 1 + 2)
    halo = []
    for i, target in ((0, left), (1, right)):
        copy = pltpu.make_async_remote_copy(
            src_ref=packed.at[i], dst_ref=edge.at[i], send_sem=halo_s.at[i], recv_sem=halo_r.at[i],
            device_id=(target, me), device_id_type=MESH,
        )
        copy.start()
        halo.append(copy)
    for i in range(EARLY):
        s_copies.append(block_copy(i))
        s_copies[-1].start()
    om_copies = []
    for k in far_first:
        peer = lax.rem(me + k, N_TM)
        copy = pltpu.make_async_remote_copy(
            src_ref=om_mine.at[peer // HALF], dst_ref=om_all.at[me],
            send_sem=om_s.at[peer], recv_sem=om_r.at[me], device_id=(tile, peer), device_id_type=MESH,
        )
        copy.start()
        om_copies.append(copy)
    om_all[me] = om_mine[half]

    for i in range(2):
        halo[i].wait_recv()
    rim_right = jnp.where(tile < n_tile - 1, edge[0].astype(F32), 0.0).astype(BF16)
    rim_left = jnp.where(tile > 0, edge[1].astype(F32), 0.0).astype(BF16)
    rim = mm(down, jnp.concatenate([rim_right, rim_left], axis=1)).astype(BF16)
    rim_buf[...] = rim
    c_copies = []
    for i in range(EARLY):
        peer = lax.rem(me + send_order[i], N_TM)
        copy = pltpu.make_async_remote_copy(
            src_ref=rim_buf.at[rows_at(peer), :], dst_ref=fix.at[i],
            send_sem=c_s.at[i], recv_sem=c_r.at[i], device_id=(tile, peer), device_id_type=MESH,
        )
        copy.start()
        c_copies.append(copy)

    def rim_matrix(g):
        rows = []
        for i in range(2):
            rows += [zeros16(16 * g, 2 * W)] if g else []
            rows += [rims[i]]
            rows += [zeros16(W - 16 * g - 16, 2 * W)] if g < FR // 2 - 1 else []
        return jnp.concatenate(rows, axis=0)

    for g in range(FR // 2):
        window = slice(2 * g * W, 2 * (g + 1) * W)
        far[:, window] = far[:, window] - mm(rim, rim_matrix(g))

    for i in range(EARLY, N_TM - 1):
        out_buf[i] = rows_of(far[rows_at(lax.rem(me + send_order[i], N_TM)), :], i % 2).astype(BF16)
        s_copies.append(block_copy(i))
        s_copies[-1].start()
    seen[:, rows_at(me), :] = rows_of(far[rows_at(me), :], 1).astype(BF16)

    time = time_ref[...].astype(F32)
    low = toeplitz(time, FRAMES, False)
    for k in range(1, N_TM):
        source = lax.rem(me + k, N_TM)
        pltpu.make_async_remote_copy(
            src_ref=om_mine.at[0], dst_ref=om_all.at[source], send_sem=om_s.at[source], recv_sem=om_r.at[source],
            device_id=(tile, source), device_id_type=MESH,
        ).wait_recv()
    om = om_all[...].astype(F32).reshape(4 * N_TM, 128)
    om = jnp.concatenate([om[:, a * K : (a + 1) * K] for a in range(4)], axis=0).astype(BF16)
    n_id = iota((FRAMES, FRAMES), 0)
    at = lax.rem(n_id, 64) // 4 * FR + n_id // 64 * 4 + lax.rem(n_id, 4)
    order = jnp.where(at == iota((FRAMES, FRAMES), 1), 1.0, 0.0).astype(BF16)
    om = mm_tn(om, order)
    orders[0] = order
    orders[1] = mm(order, low).astype(BF16)
    both = low.astype(F32) + toeplitz(time, FRAMES, True).astype(F32) - mm_tn(low, low)
    for i, part in enumerate(pieces(both, 2)):
        twice[i] = part
    probe = om - mm(om.astype(BF16), low)
    probe2 = stacked(probe, 2)

    def block_wait(i):
        source = lax.rem(me + N_TM - recv_order[i], N_TM)
        pltpu.make_async_remote_copy(
            src_ref=out_buf.at[i], dst_ref=seen.at[:, rows_at(source), :],
            send_sem=s_s.at[source], recv_sem=s_r.at[source], device_id=(tile, source), device_id_type=MESH,
        ).wait_recv()

    for copy in c_copies:
        copy.wait_recv()
    rims_in = fix[...].reshape(EARLY * SHARE, 2 * W)
    for g in range(FR // 2):
        share[:, 2 * g * W : 2 * (g + 1) * W] = mm(rims_in, rim_matrix(g))
    for i in range(EARLY):
        block_wait(i)
        window = rows_at(lax.rem(me + N_TM - recv_order[i], N_TM))
        moved = rows_of(share[i * SHARE : (i + 1) * SHARE, :], i % 2)
        seen[:, window, :] = (seen[:, window, :].astype(F32) - moved).astype(BF16)
    for i in range(EARLY, N_TM - 1):
        block_wait(i)

    def pair(i):
        return jnp.concatenate([seen[2 * i], seen[2 * i + 1]], axis=1)

    for i in range(SHARE // 2):
        y_buf[:, i * 256 : (i + 1) * 256] = stacked(fold(mm(probe2, pair(i)), 2), 2)
    pack_gram(g_mine, gram(y_buf[...]))
    x_copies = []

    def to_half(src, dst, ss, rs):
        dst[place] = src[...]
        for k in (4, 3, 5, 2, 6, 1, 7):
            other = lax.rem(place + k, HALF)
            copy = pltpu.make_async_remote_copy(
                src_ref=src, dst_ref=dst.at[place], send_sem=ss.at[other], recv_sem=rs.at[place],
                device_id=(tile, half * HALF + other), device_id_type=MESH,
            )
            copy.start()
            x_copies.append(copy)

    def from_half(src, dst, ss, rs):
        for k in range(1, HALF):
            other = lax.rem(place + k, HALF)
            pltpu.make_async_remote_copy(
                src_ref=src, dst_ref=dst.at[other], send_sem=ss.at[other], recv_sem=rs.at[other],
                device_id=(tile, half * HALF + other), device_id_type=MESH,
            ).wait_recv()

    to_half(g_mine, g_slots, g_s, g_r)
    back = jnp.zeros((2 * K, FRAMES), F32)
    for i in range(SHARE // 2):
        back = back + mm_nt(y_buf[:, i * 256 : (i + 1) * 256], pair(i))
    b_mine[...] = fold(back, 2).astype(BF16)
    to_half(b_mine, b_slots, b_s, b_r)
    from_half(g_mine, g_slots, g_s, g_r)
    g_sum = g_slots[0]
    for i in range(1, HALF):
        g_sum = g_sum + g_slots[i]
    first = inverse_factors([unpack_gram(g_sum)])[0]
    from_half(b_mine, b_slots, b_s, b_r)
    b_sum = b_slots[0].astype(F32)
    for i in range(1, HALF):
        b_sum = b_sum + b_slots[i].astype(F32)

    two = stacked(b_sum, 2)
    back = b_sum - fold(mm(two, twice[0]) + mm(two, twice[1]), 2)
    probe2 = stacked(mm(first, back, precision=HIGHEST), 2)
    for i in range(SHARE // 2):
        r = fold(mm(probe2, pair(i)), 2)
        r_buf[:, i * 256 : (i + 1) * 256] = r
        y_buf[:, i * 256 : (i + 1) * 256] = stacked(r, 2)
    pack_gram(h_mine, gram(y_buf[...]))

    own_first = [half * HALF + lax.rem(place + k, HALF) for k in (4, 3, 5, 2, 6, 1, 7)]
    own_first += [(1 - half) * HALF + lax.rem(place + k, HALF) for k in (0, 1, 7, 2, 6, 3, 5, 4)]

    def to_all(peers, src, dst, ss, rs):
        for peer in peers:
            copy = pltpu.make_async_remote_copy(
                src_ref=src(peer), dst_ref=dst.at[me], send_sem=ss.at[peer], recv_sem=rs.at[me],
                device_id=(tile, peer), device_id_type=MESH,
            )
            copy.start()
            x_copies.append(copy)

    def from_all(sources, src, dst, ss, rs):
        for source in sources:
            pltpu.make_async_remote_copy(
                src_ref=src(source), dst_ref=dst.at[source], send_sem=ss.at[source], recv_sem=rs.at[source],
                device_id=(tile, source), device_id_type=MESH,
            ).wait_recv()

    to_all(own_first[7:] + own_first[:7], lambda peer: h_mine, h_slots, h_s, h_r)
    h_slots[me] = h_mine[...]
    down_p = jnp.zeros((2 * K, FRAMES), F32)
    for i in range(SHARE // 2):
        down_p = down_p + mm_nt(y_buf[:, i * 256 : (i + 1) * 256], pair(i))
    moved = stacked(fold(down_p, 2), 2)
    moved = fold_lanes(mm_nt(orders[0], moved) - mm_nt(orders[1], moved), 2)
    moved = jnp.concatenate([moved[64 * a : 64 * a + 64] for a in range(4)], axis=1)
    d_mine[...] = moved.reshape(N_TM, 4, 4 * K).astype(BF16)
    to_all([lax.rem(me + k, N_TM) for k in far_first], lambda peer: d_mine.at[peer], d_slots, d_s, d_r)
    d_slots[me] = d_mine[me]

    def factor_of(side):
        total = h_slots[side * HALF]
        for i in range(1, HALF):
            total = total + h_slots[side * HALF + i]
        return inverse_factors([unpack_gram(total)])[0]

    def coefficients(side, factor):
        total = d_slots[side * HALF].astype(F32)
        for i in range(1, HALF):
            total = total + d_slots[side * HALF + i].astype(F32)
        coef_ref[side] = mm_nt(unpack_rows(total), factor, precision=HIGHEST)

    other = 1 - half
    for copy in halo + om_copies + s_copies + c_copies:
        copy.wait_send()
    from_all(own_first[:7], lambda peer: h_mine, h_slots, h_s, h_r)
    own = factor_of(half)
    final = own * math.sqrt(ROWS // 2 * W)
    for i in range(SHARE // 2):
        two = mm(final, r_buf[:, i * 256 : (i + 1) * 256], precision=HIGHEST)
        for j in range(2):
            basis_ref[pl.ds(2 * i + j, K, stride=SHARE), :] = two[:, j * W : (j + 1) * W]
    from_all(own_first[7:], lambda peer: h_mine, h_slots, h_s, h_r)
    distant = factor_of(other)
    from_all(own_first, lambda peer: d_mine.at[peer], d_slots, d_s, d_r)
    coefficients(half, own)
    coefficients(other, distant)

    for copy in x_copies:
        copy.wait_send()


def write_out(basis, coef, basis_out, coef_out, sems):
    copies = [pltpu.make_async_copy(basis, basis_out, sems.at[0]), pltpu.make_async_copy(coef, coef_out, sems.at[1])]
    for copy in copies:
        copy.start()
    for copy in copies:
        copy.wait()


def solution(mesh):
    n_tile = mesh.shape["tile"]

    def local(movie, omega, time_taps, space_taps):
        dma = pltpu.SemaphoreType.DMA
        vmem = pl.BlockSpec(memory_space=pltpu.VMEM)
        basis, coef = pl.pallas_call(
            functools.partial(kernel, n_tile),
            out_shape=(
                pltpu.VMEM((K * SHARE, W), F32),
                pltpu.VMEM((2, FR, K), F32),
            ),
            in_specs=[pl.BlockSpec(memory_space=pl.ANY)] * 4,
            out_specs=(vmem, vmem),
            scratch_shapes=[
                pltpu.VMEM((FR, ROWS, W), BF16),
                pltpu.VMEM((2, FR, K), BF16),
                pltpu.VMEM((2, 4, 4 * K), BF16),
                pltpu.VMEM((EARLY, SHARE, 2 * W), BF16),
                pltpu.VMEM((ROWS, 2 * W), BF16),
                pltpu.VMEM((EARLY * SHARE, FR * W), F32),
                pltpu.VMEM((1, 2 * RAD + 1), BF16),
                pltpu.VMEM((1, 2 * RAD + 1), BF16),
                pltpu.VMEM((ROWS, FR * W), F32),
                pltpu.VMEM((2, ROWS, W), BF16),
                pltpu.VMEM((2, ROWS, W), BF16),
                pltpu.VMEM((2, SHARE * FR, W), F32),
                pltpu.VMEM((N_TM, SHARE, FR, W), BF16),
                pltpu.VMEM((SHARE, FRAMES, W), BF16),
                pltpu.VMEM((N_TM, 4, 4 * K), BF16),
                pltpu.VMEM((HALF, K, FRAMES), BF16),
                pltpu.VMEM((HALF, 8, 128), F32),
                pltpu.VMEM((K, FRAMES), BF16),
                pltpu.VMEM((8, 128), F32),
                pltpu.VMEM((2, FRAMES, FRAMES), BF16),
                pltpu.VMEM((2, FRAMES, FRAMES), BF16),
                pltpu.VMEM((8, 128), F32),
                pltpu.VMEM((N_TM, 8, 128), F32),
                pltpu.VMEM((N_TM, 4, 4 * K), BF16),
                pltpu.VMEM((N_TM, 4, 4 * K), BF16),
                pltpu.VMEM((2 * K, PIX), BF16),
                pltpu.VMEM((K, PIX), F32),
                dma((4,)), dma((2,)), dma((2,)), dma((N_TM,)), dma((N_TM,)), dma((N_TM,)), dma((N_TM,)),
                dma((EARLY,)), dma((EARLY,)),
                dma((HALF,)), dma((HALF,)), dma((HALF,)), dma((HALF,)),
                dma((N_TM,)), dma((N_TM,)), dma((N_TM,)), dma((N_TM,)),
            ],
            compiler_params=pltpu.CompilerParams(collective_id=0, has_side_effects=True),
            name="low_rank",
        )(
            movie,
            jnp.transpose(omega[:, 0], (0, 2, 1)),
            time_taps.reshape(1, -1),
            space_taps.reshape(1, -1),
        )
        basis, coef = pl.pallas_call(
            write_out,
            out_shape=(
                jax.ShapeDtypeStruct((K * SHARE, W), F32),
                jax.ShapeDtypeStruct((2, FR, K), F32),
            ),
            in_specs=[pl.BlockSpec(memory_space=pltpu.VMEM)] * 2,
            out_specs=(pl.BlockSpec(memory_space=pl.ANY),) * 2,
            scratch_shapes=[dma((2,))],
            name="write_out",
        )(pltpu.with_memory_space_constraint(basis, pltpu.VMEM), pltpu.with_memory_space_constraint(coef, pltpu.VMEM))
        return basis.reshape(K, SHARE, W), jnp.transpose(coef, (0, 2, 1))[:, None]

    in_specs = (P("tm", None, "tile"), P(None, "tile", None, "tm"), P(), P())
    out_specs = (P(None, "tm", "tile"), P(None, "tile", None, "tm"))
    return jax.shard_map(local, mesh=mesh, in_specs=in_specs, out_specs=out_specs, check_vma=False)
```

```python
import functools
import math

import jax
import jax.numpy as jnp
from jax import lax
from jax.experimental import pallas as pl
from jax.experimental.pallas import tpu as pltpu
from jax.sharding import PartitionSpec as P

MESH = pl.DeviceIdType.MESH
F32 = jnp.float32
BF16 = jnp.bfloat16
HIGHEST = lax.Precision.HIGHEST

N_TM = 16
HALF = 8
FR = 16
FRAMES = 256
ROWS = 256
SHARE = 16
W = 128
K = 32
RAD = 8
PIX = SHARE * W
EARLY = 2


def mm(a, b, **kw):
    return jnp.dot(a, b, preferred_element_type=F32, **kw)


def mm_nt(a, b, **kw):
    return lax.dot_general(a, b, (((1,), (1,)), ((), ())), preferred_element_type=F32, **kw)


def mm_tn(a, b, **kw):
    return lax.dot_general(a, b, (((0,), (0,)), ((), ())), preferred_element_type=F32, **kw)


def pieces(x, count):
    out = []
    for _ in range(count - 1):
        part = x.astype(BF16)
        out.append(part)
        x = x - part.astype(F32)
    out.append(x.astype(BF16))
    return out


def stacked(x, count, axis=0):
    return jnp.concatenate(pieces(x, count), axis=axis)


def fold(x, count):
    total = x[:K]
    for i in range(1, count):
        total = total + x[i * K : (i + 1) * K]
    return total


def fold_lanes(x, count):
    total = x[:, :K]
    for i in range(1, count):
        total = total + x[:, i * K : (i + 1) * K]
    return total


def iota(shape, dim):
    return lax.broadcasted_iota(jnp.int32, shape, dim)


def from_taps(taps, index):
    out = jnp.zeros(index.shape, F32)
    for k in range(2 * RAD + 1):
        out = jnp.where(index == k, taps[:, k : k + 1], out)
    return out


def gram(x2):
    return fold_lanes(fold(mm_nt(x2, x2), 2), 2)


def inverse_factors(grams):
    row = iota((8, 128), 0)
    eye = jnp.where(iota((K, K), 0) == iota((K, K), 1), 1.0, 0.0)
    state = []
    for g in grams:
        aug = jnp.concatenate([g, eye, jnp.zeros((K, 64), F32)], axis=1)
        state.append(([aug[8 * i : 8 * i + 8] for i in range(4)], []))
    for b in range(4):
        spread = [
            [[jnp.broadcast_to(aug[i][:, 8 * b + t : 8 * b + t + 1], (8, 128)) for i in range(b, 4)] for t in range(8)]
            for aug, _ in state
        ]
        scale = [jnp.ones((8, 128), F32) for _ in state]
        for t in range(8):
            for n, (aug, _) in enumerate(state):
                cols = spread[n]
                pivot = cols[t][0][t : t + 1, :]
                inverse = 1.0 / pivot
                scale[n] = jnp.where(row == t, pivot, scale[n])
                line = aug[b][t : t + 1, :] * inverse
                heads = [cols[u][0][t : t + 1, :] * inverse for u in range(t + 1, 8)]
                for i in range(b, 4):
                    factor = cols[t][i - b]
                    if i == b:
                        factor = jnp.where(row > t, factor, 0.0)
                    aug[i] = aug[i] - factor * line
                    for u in range(t + 1, 8):
                        cols[u][i - b] = cols[u][i - b] - factor * heads[u - t - 1]
        for n, (aug, done) in enumerate(state):
            done.append(aug[b] * lax.rsqrt(scale[n]))
    return [jnp.concatenate(done, axis=0)[:, K : 2 * K] for _, done in state]


def toeplitz(taps, size, flip):
    lane, row = iota((8, size), 1), iota((8, size), 0)
    head = from_taps(taps, row + 2 * RAD - lane if flip else lane - row)
    rows = []
    for i in range(size // 8):
        block = head
        if i == 0:
            block = jnp.where(lane >= 8, head, 0.0)
        if i == size // 8 - 1:
            block = jnp.where(lane < 16, head, 0.0)
        shift = (8 * i - 8) % size
        rows.append(pltpu.roll(block, shift, 1) if shift else block)
    return jnp.concatenate(rows, axis=0).astype(BF16)


def zeros16(*shape):
    return jnp.zeros(shape, BF16)


def pack_gram(ref, g):
    for i in range(4):
        ref[:, i * K : (i + 1) * K] = g[8 * i : 8 * i + 8, :]


def unpack_rows(total):
    return jnp.concatenate([total[:, i * K : (i + 1) * K] for i in range(4)], axis=0)


def unpack_gram(total):
    return jnp.concatenate([total[:, i * K : (i + 1) * K] for i in range(4)], axis=0)


def kernel(
    n_tile,
    movie_hbm, omega_hbm, time_hbm, space_hbm,
    basis_ref, coef_ref,
    movie, omega_ref, om_mine, fix, rim_buf, share, time_ref, space_ref, far, packed, edge, turn, out_buf, seen, om_all,
    b_slots, g_slots, b_mine, b_half, b_swap, g_mine, orders, twice, h_mine, h_slots, d_mine, d_slots, y_buf, r_buf,
    load_sem, halo_s, halo_r, s_s, s_r, om_s, om_r, c_s, c_r, w_s, w_r, b_s, b_r, g_s, g_r, h_s, h_r, d_s, d_r,
):
    tile = lax.axis_index("tile")
    me = lax.axis_index("tm")
    half = me // HALF
    place = me - half * HALF
    left = lax.rem(tile + n_tile - 1, n_tile)
    right = lax.rem(tile + 1, n_tile)
    far_first = (8, 7, 9, 6, 10, 5, 11, 4, 12, 3, 13, 2, 14, 1, 15)
    core = lax.rem(me, 2)
    send_order = (8, 7 + 2 * core, 9 - 2 * core) + far_first[3:]
    recv_order = (8, 9 - 2 * core, 7 + 2 * core) + far_first[3:]

    loads = [
        pltpu.make_async_copy(src, dst, load_sem.at[i])
        for i, (src, dst) in enumerate(
            ((movie_hbm, movie), (space_hbm, space_ref), (time_hbm, time_ref), (omega_hbm, omega_ref))
        )
    ]
    for load in loads:
        load.start()
    barrier = pltpu.get_barrier_semaphore()
    for k in far_first:
        pl.semaphore_signal(barrier, inc=1, device_id=(tile, lax.rem(me + k, N_TM)), device_id_type=MESH)
    pl.semaphore_signal(barrier, inc=1, device_id=(left, me), device_id_type=MESH)
    pl.semaphore_signal(barrier, inc=1, device_id=(right, me), device_id_type=MESH)

    loads[1].wait()
    space = space_ref[...].astype(F32)
    down = toeplitz(space, ROWS, False)
    side = toeplitz(space, W, True)
    across = jnp.concatenate(
        [jnp.concatenate([side, zeros16(W, W)], axis=1), jnp.concatenate([zeros16(W, W), side], axis=1)], axis=0
    )
    lane8, row8 = iota((8, W), 1), iota((8, W), 0)
    none8 = jnp.zeros((8, W), F32)
    rims = []
    for offset in (136, 0):
        one = from_taps(space, offset + row8 - lane8)
        rims.append(
            jnp.concatenate(
                [jnp.concatenate([one, none8], axis=1), jnp.concatenate([none8, one], axis=1)], axis=0
            ).astype(BF16)
        )
    unit = jnp.where(lane8 == row8, 1.0, 0.0)
    picks = []
    for f in range(FR):
        moved = pltpu.roll(unit, 8 * f, 1) if f else unit
        top = jnp.concatenate([moved, none8], axis=0).astype(BF16)
        bottom = jnp.concatenate([none8, moved], axis=0).astype(BF16)
        picks.append(jnp.concatenate([top, zeros16(16, W)], axis=1))
        picks.append(zeros16(W - 32, 2 * W))
        picks.append(jnp.concatenate([zeros16(16, W), bottom], axis=1))
    loads[0].wait()

    def frames2(g):
        return jnp.concatenate([movie[2 * g], movie[2 * g + 1]], axis=1)

    total = mm(jnp.concatenate([movie[f] for f in range(FR)], axis=1), jnp.concatenate(picks, axis=0))
    packed[0] = total[:, :W].astype(BF16)
    packed[1] = total[:, W:].astype(BF16)

    for g in range(FR // 2):
        two = frames2(g)
        mid = mm(down, two).astype(BF16)
        far[:, 2 * g * W : 2 * (g + 1) * W] = two.astype(F32) - mm(mid, across)


    def rows_of(values, slot):
        for f in range(FR):
            turn[slot, pl.ds(f, SHARE, stride=FR), :] = values[:, f * W : (f + 1) * W]
        return turn[slot].reshape(SHARE, FR, W)

    def rows_at(peer):
        return pl.ds(pl.multiple_of(peer * SHARE, SHARE), SHARE)

    s_copies = []

    def block_copy(i):
        peer = lax.rem(me + send_order[i], N_TM)
        return pltpu.make_async_remote_copy(
            src_ref=out_buf.at[i], dst_ref=seen.at[:, rows_at(me), :],
            send_sem=s_s.at[peer], recv_sem=s_r.at[me], device_id=(tile, peer), device_id_type=MESH,
        )

    for i in range(EARLY):
        out_buf[i] = rows_of(far[rows_at(lax.rem(me + send_order[i], N_TM)), :], i % 2).astype(BF16)
    loads[2].wait()
    loads[3].wait()
    for i in range(2):
        some = omega_ref[i].astype(F32)
        om_mine[i] = jnp.concatenate([some[4 * a : 4 * a + 4] for a in range(4)], axis=1).astype(BF16)

    pl.semaphore_wait(barrier, N_TM - 1 + 2)
    halo = []
    for i, target in ((0, left), (1, right)):
        copy = pltpu.make_async_remote_copy(
            src_ref=packed.at[i], dst_ref=edge.at[i], send_sem=halo_s.at[i], recv_sem=halo_r.at[i],
            device_id=(target, me), device_id_type=MESH,
        )
        copy.start()
        halo.append(copy)
    for i in range(EARLY):
        s_copies.append(block_copy(i))
        s_copies[-1].start()
    om_copies = []
    for k in far_first:
        peer = lax.rem(me + k, N_TM)
        copy = pltpu.make_async_remote_copy(
            src_ref=om_mine.at[peer // HALF], dst_ref=om_all.at[me],
            send_sem=om_s.at[peer], recv_sem=om_r.at[me], device_id=(tile, peer), device_id_type=MESH,
        )
        copy.start()
        om_copies.append(copy)
    om_all[me] = om_mine[half]

    for i in range(2):
        halo[i].wait_recv()
    rim_right = jnp.where(tile < n_tile - 1, edge[0].astype(F32), 0.0).astype(BF16)
    rim_left = jnp.where(tile > 0, edge[1].astype(F32), 0.0).astype(BF16)
    rim = mm(down, jnp.concatenate([rim_right, rim_left], axis=1)).astype(BF16)
    rim_buf[...] = rim
    c_copies = []
    for i in range(EARLY):
        peer = lax.rem(me + send_order[i], N_TM)
        copy = pltpu.make_async_remote_copy(
            src_ref=rim_buf.at[rows_at(peer), :], dst_ref=fix.at[i],
            send_sem=c_s.at[i], recv_sem=c_r.at[i], device_id=(tile, peer), device_id_type=MESH,
        )
        copy.start()
        c_copies.append(copy)

    def rim_matrix(g):
        rows = []
        for i in range(2):
            rows += [zeros16(16 * g, 2 * W)] if g else []
            rows += [rims[i]]
            rows += [zeros16(W - 16 * g - 16, 2 * W)] if g < FR // 2 - 1 else []
        return jnp.concatenate(rows, axis=0)

    for g in range(FR // 2):
        window = slice(2 * g * W, 2 * (g + 1) * W)
        far[:, window] = far[:, window] - mm(rim, rim_matrix(g))

    for i in range(EARLY, N_TM - 1):
        out_buf[i] = rows_of(far[rows_at(lax.rem(me + send_order[i], N_TM)), :], i % 2).astype(BF16)
        s_copies.append(block_copy(i))
        s_copies[-1].start()
    seen[:, rows_at(me), :] = rows_of(far[rows_at(me), :], 1).astype(BF16)

    time = time_ref[...].astype(F32)
    low = toeplitz(time, FRAMES, False)
    for k in range(1, N_TM):
        source = lax.rem(me + k, N_TM)
        pltpu.make_async_remote_copy(
            src_ref=om_mine.at[0], dst_ref=om_all.at[source], send_sem=om_s.at[source], recv_sem=om_r.at[source],
            device_id=(tile, source), device_id_type=MESH,
        ).wait_recv()
    om = om_all[...].astype(F32).reshape(4 * N_TM, 128)
    om = jnp.concatenate([om[:, a * K : (a + 1) * K] for a in range(4)], axis=0).astype(BF16)
    n_id = iota((FRAMES, FRAMES), 0)
    at = lax.rem(n_id, 64) // 4 * FR + n_id // 64 * 4 + lax.rem(n_id, 4)
    order = jnp.where(at == iota((FRAMES, FRAMES), 1), 1.0, 0.0).astype(BF16)
    om = mm_tn(om, order)
    orders[0] = order
    orders[1] = mm(order, low).astype(BF16)
    both = low.astype(F32) + toeplitz(time, FRAMES, True).astype(F32) - mm_tn(low, low)
    for i, part in enumerate(pieces(both, 2)):
        twice[i] = part
    probe = om - mm(om.astype(BF16), low)
    probe2 = stacked(probe, 2)

    def block_wait(i):
        source = lax.rem(me + N_TM - recv_order[i], N_TM)
        pltpu.make_async_remote_copy(
            src_ref=out_buf.at[i], dst_ref=seen.at[:, rows_at(source), :],
            send_sem=s_s.at[source], recv_sem=s_r.at[source], device_id=(tile, source), device_id_type=MESH,
        ).wait_recv()

    for copy in c_copies:
        copy.wait_recv()
    rims_in = fix[...].reshape(EARLY * SHARE, 2 * W)
    for g in range(FR // 2):
        share[:, 2 * g * W : 2 * (g + 1) * W] = mm(rims_in, rim_matrix(g))
    for i in range(EARLY):
        block_wait(i)
        window = rows_at(lax.rem(me + N_TM - recv_order[i], N_TM))
        moved = rows_of(share[i * SHARE : (i + 1) * SHARE, :], i % 2)
        seen[:, window, :] = (seen[:, window, :].astype(F32) - moved).astype(BF16)
    for i in range(EARLY, N_TM - 1):
        block_wait(i)

    def pair(i):
        return jnp.concatenate([seen[2 * i], seen[2 * i + 1]], axis=1)

    for i in range(SHARE // 2):
        y_buf[:, i * 256 : (i + 1) * 256] = stacked(fold(mm(probe2, pair(i)), 2), 2)
    pack_gram(g_mine, gram(y_buf[...]))
    x_copies = []

    def to_half(src, dst, ss, rs):
        for k in (4, 3, 5, 2, 6, 1, 7):
            other = lax.rem(place + k, HALF)
            copy = pltpu.make_async_remote_copy(
                src_ref=src(other), dst_ref=dst.at[place], send_sem=ss.at[other], recv_sem=rs.at[place],
                device_id=(tile, half * HALF + other), device_id_type=MESH,
            )
            copy.start()
            x_copies.append(copy)

    def from_half(src, dst, ss, rs):
        for k in range(1, HALF):
            other = lax.rem(place + k, HALF)
            pltpu.make_async_remote_copy(
                src_ref=src(other), dst_ref=dst.at[other], send_sem=ss.at[other], recv_sem=rs.at[other],
                device_id=(tile, half * HALF + other), device_id_type=MESH,
            ).wait_recv()

    to_half(lambda other: g_mine, g_slots, g_s, g_r)
    g_slots[place] = g_mine[...]
    back = jnp.zeros((2 * K, FRAMES), F32)
    for i in range(SHARE // 2):
        back = back + mm_nt(y_buf[:, i * 256 : (i + 1) * 256], pair(i))
    back = fold(back, 2).astype(BF16)
    for i in range(2):
        b_mine[i] = back[:, i * W : (i + 1) * W]

    def half_for(other):
        return b_mine.at[lax.rem(other, 2)]

    to_half(half_for, b_slots, b_s, b_r)
    b_slots[place] = b_mine[core]
    from_half(lambda other: g_mine, g_slots, g_s, g_r)
    g_sum = g_slots[0]
    for i in range(1, HALF):
        g_sum = g_sum + g_slots[i]
    first = inverse_factors([unpack_gram(g_sum)])[0]
    from_half(half_for, b_slots, b_s, b_r)
    b_sum = b_slots[0].astype(F32)
    for i in range(1, HALF):
        b_sum = b_sum + b_slots[i].astype(F32)
    b_half[...] = b_sum
    swap = pltpu.make_async_remote_copy(
        src_ref=b_half, dst_ref=b_swap, send_sem=w_s, recv_sem=w_r,
        device_id=(tile, me + 1 - 2 * core), device_id_type=MESH,
    )
    swap.start()
    swap.wait_recv()
    x_copies.append(swap)
    given = b_swap[...]
    b_sum = jnp.where(core == 0, jnp.concatenate([b_sum, given], axis=1), jnp.concatenate([given, b_sum], axis=1))

    two = stacked(b_sum, 2)
    back = b_sum - fold(mm(two, twice[0]) + mm(two, twice[1]), 2)
    probe2 = stacked(mm(first, back, precision=HIGHEST), 2)
    for i in range(SHARE // 2):
        r = fold(mm(probe2, pair(i)), 2)
        r_buf[:, i * 256 : (i + 1) * 256] = r
        y_buf[:, i * 256 : (i + 1) * 256] = stacked(r, 2)
    pack_gram(h_mine, gram(y_buf[...]))

    own_first = [half * HALF + lax.rem(place + k, HALF) for k in (4, 3, 5, 2, 6, 1, 7)]
    own_first += [(1 - half) * HALF + lax.rem(place + k, HALF) for k in (0, 1, 7, 2, 6, 3, 5, 4)]

    def to_all(peers, src, dst, ss, rs):
        for peer in peers:
            copy = pltpu.make_async_remote_copy(
                src_ref=src(peer), dst_ref=dst.at[me], send_sem=ss.at[peer], recv_sem=rs.at[me],
                device_id=(tile, peer), device_id_type=MESH,
            )
            copy.start()
            x_copies.append(copy)

    def from_all(sources, src, dst, ss, rs):
        for source in sources:
            pltpu.make_async_remote_copy(
                src_ref=src(source), dst_ref=dst.at[source], send_sem=ss.at[source], recv_sem=rs.at[source],
                device_id=(tile, source), device_id_type=MESH,
            ).wait_recv()

    to_all(own_first[7:] + own_first[:7], lambda peer: h_mine, h_slots, h_s, h_r)
    h_slots[me] = h_mine[...]
    down_p = jnp.zeros((2 * K, FRAMES), F32)
    for i in range(SHARE // 2):
        down_p = down_p + mm_nt(y_buf[:, i * 256 : (i + 1) * 256], pair(i))
    moved = stacked(fold(down_p, 2), 2)
    moved = fold_lanes(mm_nt(orders[0], moved) - mm_nt(orders[1], moved), 2)
    moved = jnp.concatenate([moved[64 * a : 64 * a + 64] for a in range(4)], axis=1)
    d_mine[...] = moved.reshape(N_TM, 4, 4 * K).astype(BF16)
    to_all([lax.rem(me + k, N_TM) for k in far_first], lambda peer: d_mine.at[peer], d_slots, d_s, d_r)
    d_slots[me] = d_mine[me]

    def factor_of(side):
        total = h_slots[side * HALF]
        for i in range(1, HALF):
            total = total + h_slots[side * HALF + i]
        return inverse_factors([unpack_gram(total)])[0]

    def coefficients(side, factor):
        total = d_slots[side * HALF].astype(F32)
        for i in range(1, HALF):
            total = total + d_slots[side * HALF + i].astype(F32)
        coef_ref[side] = mm_nt(unpack_rows(total), factor, precision=HIGHEST)

    other = 1 - half
    for copy in halo + om_copies + s_copies + c_copies:
        copy.wait_send()
    from_all(own_first[:7], lambda peer: h_mine, h_slots, h_s, h_r)
    own = factor_of(half)
    final = own * math.sqrt(ROWS // 2 * W)
    for i in range(SHARE // 2):
        two = mm(final, r_buf[:, i * 256 : (i + 1) * 256], precision=HIGHEST)
        for j in range(2):
            basis_ref[pl.ds(2 * i + j, K, stride=SHARE), :] = two[:, j * W : (j + 1) * W]
    from_all(own_first[7:], lambda peer: h_mine, h_slots, h_s, h_r)
    distant = factor_of(other)
    from_all(own_first, lambda peer: d_mine.at[peer], d_slots, d_s, d_r)
    coefficients(half, own)
    coefficients(other, distant)

    for copy in x_copies:
        copy.wait_send()


def write_out(basis, coef, basis_out, coef_out, sems):
    copies = [pltpu.make_async_copy(basis, basis_out, sems.at[0]), pltpu.make_async_copy(coef, coef_out, sems.at[1])]
    for copy in copies:
        copy.start()
    for copy in copies:
        copy.wait()


def solution(mesh):
    n_tile = mesh.shape["tile"]

    def local(movie, omega, time_taps, space_taps):
        dma = pltpu.SemaphoreType.DMA
        vmem = pl.BlockSpec(memory_space=pltpu.VMEM)
        basis, coef = pl.pallas_call(
            functools.partial(kernel, n_tile),
            out_shape=(
                pltpu.VMEM((K * SHARE, W), F32),
                pltpu.VMEM((2, FR, K), F32),
            ),
            in_specs=[pl.BlockSpec(memory_space=pl.ANY)] * 4,
            out_specs=(vmem, vmem),
            scratch_shapes=[
                pltpu.VMEM((FR, ROWS, W), BF16),
                pltpu.VMEM((2, FR, K), BF16),
                pltpu.VMEM((2, 4, 4 * K), BF16),
                pltpu.VMEM((EARLY, SHARE, 2 * W), BF16),
                pltpu.VMEM((ROWS, 2 * W), BF16),
                pltpu.VMEM((EARLY * SHARE, FR * W), F32),
                pltpu.VMEM((1, 2 * RAD + 1), BF16),
                pltpu.VMEM((1, 2 * RAD + 1), BF16),
                pltpu.VMEM((ROWS, FR * W), F32),
                pltpu.VMEM((2, ROWS, W), BF16),
                pltpu.VMEM((2, ROWS, W), BF16),
                pltpu.VMEM((2, SHARE * FR, W), F32),
                pltpu.VMEM((N_TM, SHARE, FR, W), BF16),
                pltpu.VMEM((SHARE, FRAMES, W), BF16),
                pltpu.VMEM((N_TM, 4, 4 * K), BF16),
                pltpu.VMEM((HALF, K, W), BF16),
                pltpu.VMEM((HALF, 8, 128), F32),
                pltpu.VMEM((2, K, W), BF16),
                pltpu.VMEM((K, W), F32),
                pltpu.VMEM((K, W), F32),
                pltpu.VMEM((8, 128), F32),
                pltpu.VMEM((2, FRAMES, FRAMES), BF16),
                pltpu.VMEM((2, FRAMES, FRAMES), BF16),
                pltpu.VMEM((8, 128), F32),
                pltpu.VMEM((N_TM, 8, 128), F32),
                pltpu.VMEM((N_TM, 4, 4 * K), BF16),
                pltpu.VMEM((N_TM, 4, 4 * K), BF16),
                pltpu.VMEM((2 * K, PIX), BF16),
                pltpu.VMEM((K, PIX), F32),
                dma((4,)), dma((2,)), dma((2,)), dma((N_TM,)), dma((N_TM,)), dma((N_TM,)), dma((N_TM,)),
                dma((EARLY,)), dma((EARLY,)), dma(()), dma(()),
                dma((HALF,)), dma((HALF,)), dma((HALF,)), dma((HALF,)),
                dma((N_TM,)), dma((N_TM,)), dma((N_TM,)), dma((N_TM,)),
            ],
            compiler_params=pltpu.CompilerParams(collective_id=0, has_side_effects=True),
            name="low_rank",
        )(
            movie,
            jnp.transpose(omega[:, 0], (0, 2, 1)),
            time_taps.reshape(1, -1),
            space_taps.reshape(1, -1),
        )
        basis, coef = pl.pallas_call(
            write_out,
            out_shape=(
                jax.ShapeDtypeStruct((K * SHARE, W), F32),
                jax.ShapeDtypeStruct((2, FR, K), F32),
            ),
            in_specs=[pl.BlockSpec(memory_space=pltpu.VMEM)] * 2,
            out_specs=(pl.BlockSpec(memory_space=pl.ANY),) * 2,
            scratch_shapes=[dma((2,))],
            name="write_out",
        )(pltpu.with_memory_space_constraint(basis, pltpu.VMEM), pltpu.with_memory_space_constraint(coef, pltpu.VMEM))
        return basis.reshape(K, SHARE, W), jnp.transpose(coef, (0, 2, 1))[:, None]

    in_specs = (P("tm", None, "tile"), P(None, "tile", None, "tm"), P(), P())
    out_specs = (P(None, "tm", "tile"), P(None, "tile", None, "tm"))
    return jax.shard_map(local, mesh=mesh, in_specs=in_specs, out_specs=out_specs, check_vma=False)
```
